32 devices in a mesh: row: 4 (over y, x), col: 8 (over z, core).
Axes of the slice: x: 2, y: 2, z: 4, core: 2. Of those that a mesh axis runs over, the one named last changes fastest.
Arguments:
- tokens: bfloat16 [256, 8192], P('col', 'row'), may hold values from -500 to 500
- norm_gain: float32 [8192], P('row'), may hold values from 0.5 to 1.5
- cotangent: bfloat16 [256, 8192], P('col', 'row'), may hold values from -6 to 6
- gate_frozen_weight: bfloat16 [8192, 28672], P('row', 'col'), may hold values from -0.0625 to 0.0625
- up_frozen_weight: bfloat16 [8192, 28672], P('row', 'col'), may hold values from -0.0625 to 0.0625
- down_frozen_weight: bfloat16 [28672, 8192], P('col', 'row'), may hold values from -0.03125 to 0.03125
- gate_input_factor: bfloat16 [8192, 64], P('row'), may hold values from -0.0625 to 0.0625
- gate_output_factor: bfloat16 [64, 28672], P(None, 'col'), may hold values from -0.75 to 0.75
- up_input_factor: bfloat16 [8192, 64], P('row'), may hold values from -0.0625 to 0.0625
- up_output_factor: bfloat16 [64, 28672], P(None, 'col'), may hold values from -0.75 to 0.75
- down_input_factor: bfloat16 [28672, 64], P('col'), may hold values from -0.03125 to 0.03125
- down_b: bfloat16 [64, 8192], P(None, 'row'), may hold values from -0.75 to 0.75
- gate_input_factor_direction: bfloat16 [8192, 64], P('row'), may hold values from -0.0625 to 0.0625
- gate_output_factor_direction: bfloat16 [64, 28672], P(None, 'col'), may hold values from -0.75 to 0.75
- up_input_factor_direction: bfloat16 [8192, 64], P('row'), may hold values from -0.0625 to 0.0625
- up_output_factor_direction: bfloat16 [64, 28672], P(None, 'col'), may hold values from -0.75 to 0.75
- down_input_factor_direction: bfloat16 [28672, 64], P('col'), may hold values from -0.03125 to 0.03125
- down_b_dir: bfloat16 [64, 8192], P(None, 'row'), may hold values from -0.75 to 0.75
Outputs:
- normed_feature_adjoint: float32 [256, 8192], P('col', 'row')
- normed_feature_adjoint_direction: float32 [256, 8192], P('col', 'row')
- curvature_gate_input: float32 [8192, 64], P('row')
- curvature_gate_output: float32 [64, 28672], P(None, 'col')
- curvature_up_input: float32 [8192, 64], P('row')
- curvature_up_output: float32 [64, 28672], P(None, 'col')
- curvature_down_input: float32 [28672, 64], P('col')
- curvature_down_output: float32 [64, 8192], P(None, 'row')
The draws below stay inside these ranges and needn't reach their ends.
All inputs are finite; a program needn't handle non-finite values.
Results may differ from the reference program's by a relative error of at most 0.024.
Values may be sent and summed in bfloat16 or wider, within the bound.
A program may use at most 128 MiB of HBM per device.

```python
import jax
import jax.numpy as jnp
from jax import lax

D = 8192
FF = 28672
R = 64
TOKENS = 256


def draw_tokens(key, part):
    base_key = jax.random.fold_in(key, 11)
    noise_key, column_key, row_key = jax.random.split(base_key, 3)
    position = jnp.arange(D, dtype=jnp.float32) / D
    column_scale = jnp.power(10.0, 0.6 * position + 0.4 * jax.random.uniform(column_key, (D,), jnp.float32))
    values = jnp.clip(jax.random.normal(noise_key, (TOKENS, D), jnp.float32), -4.0, 4.0)
    row_scale = jnp.power(10.0, jax.random.uniform(row_key, (TOKENS, 1), jnp.float32))
    return (values * row_scale * column_scale).astype(jnp.bfloat16)


def shard_levels(stream_key, dims, cuts, least, top_value):
    factor_of = 1.0
    for axis_at, shards_of in cuts:
        heights = jax.random.uniform(jax.random.fold_in(jax.random.fold_in(stream_key, 6), axis_at), (shards_of,), jnp.float32, least / len(cuts), top_value / len(cuts))
        factor_of = factor_of * jnp.repeat(jnp.exp(heights), dims[axis_at] // shards_of).reshape((-1,) + (1,) * (len(dims) - 1 - axis_at))
    return factor_of


def scatter_about(key, shape, deviation, bound, cuts=(), held_as=jnp.bfloat16):
    values = deviation * jax.random.normal(key, shape, jnp.float32)
    if cuts:
        values = values * shard_levels(key, shape, cuts, -0.22, 0.18)
    return jnp.clip(values, -bound, bound).astype(held_as)


def setup_inputs(seed: int = 0) -> dict:
    key_of = jax.random.split(jax.random.key(seed), 19)
    return {
        "tokens": draw_tokens(jax.random.fold_in(key_of[18], 71), 0),
        "norm_gain": jnp.clip(1.0 + 0.1 * jax.random.normal(key_of[1], (D,), jnp.float32), 0.5, 1.5),
        "cotangent": scatter_about(key_of[2], (TOKENS, D), 1.0, 6.0, ((0, 8), (1, 4))),
        "gate_frozen_weight": scatter_about(key_of[3], (D, FF), D ** -0.5, 0.0625, ((0, 4), (1, 8))),
        "up_frozen_weight": scatter_about(key_of[4], (D, FF), D ** -0.5, 0.0625, ((0, 4), (1, 8))),
        "down_frozen_weight": scatter_about(key_of[5], (FF, D), FF ** -0.5, 0.03125, ((0, 8), (1, 4))),
        "gate_input_factor": scatter_about(key_of[6], (D, R), D ** -0.5, 0.0625, ((0, 4),)),
        "gate_output_factor": scatter_about(key_of[7], (R, FF), R ** -0.5, 0.75, ((1, 8),)),
        "up_input_factor": scatter_about(key_of[8], (D, R), D ** -0.5, 0.0625, ((0, 4),)),
        "up_output_factor": scatter_about(key_of[9], (R, FF), R ** -0.5, 0.75, ((1, 8),)),
        "down_input_factor": scatter_about(key_of[10], (FF, R), FF ** -0.5, 0.03125, ((0, 8),)),
        "down_b": scatter_about(key_of[11], (R, D), R ** -0.5, 0.75, ((1, 4),)),
        "gate_input_factor_direction": scatter_about(key_of[12], (D, R), D ** -0.5, 0.0625, ((0, 4),)),
        "gate_output_factor_direction": scatter_about(key_of[13], (R, FF), R ** -0.5, 0.75, ((1, 8),)),
        "up_input_factor_direction": scatter_about(key_of[14], (D, R), D ** -0.5, 0.0625, ((0, 4),)),
        "up_output_factor_direction": scatter_about(key_of[15], (R, FF), R ** -0.5, 0.75, ((1, 8),)),
        "down_input_factor_direction": scatter_about(key_of[16], (FF, R), FF ** -0.5, 0.03125, ((0, 8),)),
        "down_b_dir": scatter_about(key_of[17], (R, D), R ** -0.5, 0.75, ((1, 4),)),
    }


adapter_scale = 0.5
epsilon = 1e-05

def curvature_product(left, right):
    return jnp.dot(left, right, preferred_element_type=jnp.float32)

def cross_shard_total(left, right):
    return lax.dot_general(left, right, (((1,), (1,)), ((), ())), preferred_element_type=jnp.float32)

def summed_over_rows(left, right):
    return lax.dot_general(left, right, (((0,), (0,)), ((), ())), preferred_element_type=jnp.float32)

def exact_row_values(left, right):
    return lax.dot_general(left.astype(jnp.float32), right.astype(jnp.float32), (((0,), (0,)), ((), ())), precision=lax.Precision.HIGHEST)

def exact_cross_total(left, right):
    return lax.dot_general(left.astype(jnp.float32), right.astype(jnp.float32), (((1,), (1,)), ((), ())), precision=lax.Precision.HIGHEST)

def second_order(gate_preactivation, up_preactivation, hidden_adjoint, gate_tangent_rows, up_tangent_rows, adjoint_tangent_rows):
    sigma = jax.nn.sigmoid(gate_preactivation)
    silu_value = gate_preactivation * sigma
    slope = sigma * (1.0 + gate_preactivation * (1.0 - sigma))
    bend = sigma * (1.0 - sigma) * (2.0 + gate_preactivation * (1.0 - 2.0 * sigma))
    hidden_activation = (silu_value * up_preactivation).astype(jnp.bfloat16)
    hidden_direction = (slope * gate_tangent_rows * up_preactivation + silu_value * up_tangent_rows).astype(jnp.bfloat16)
    gate_derivative = (hidden_adjoint * up_preactivation * slope).astype(jnp.bfloat16)
    up_derivative = (hidden_adjoint * silu_value).astype(jnp.bfloat16)
    gate_derivative_direction = (adjoint_tangent_rows * up_preactivation * slope + hidden_adjoint * (up_tangent_rows * slope + up_preactivation * bend * gate_tangent_rows)).astype(jnp.bfloat16)
    up_derivative_direction = (adjoint_tangent_rows * silu_value + hidden_adjoint * slope * gate_tangent_rows).astype(jnp.bfloat16)
    return (hidden_activation, hidden_direction, gate_derivative, up_derivative, gate_derivative_direction, up_derivative_direction)

def reference(tokens, norm_gain, cotangent, gate_frozen_weight, up_frozen_weight, down_frozen_weight, gate_input_factor, gate_output_factor, up_input_factor, up_output_factor, down_input_factor, down_b, gate_input_factor_direction, gate_output_factor_direction, up_input_factor_direction, up_output_factor_direction, down_input_factor_direction, down_b_dir):
    tokens_f = tokens.astype(jnp.float32)
    inv_rms = lax.rsqrt(lax.optimization_barrier(jnp.sum(tokens_f * tokens_f, axis=1, keepdims=True)) / D + epsilon)
    normed_tokens = (tokens_f * inv_rms * norm_gain).astype(jnp.bfloat16)
    ranks = jnp.concatenate([curvature_product(normed_tokens, gate_input_factor), curvature_product(normed_tokens, up_input_factor), curvature_product(normed_tokens, gate_input_factor_direction), curvature_product(normed_tokens, up_input_factor_direction), cross_shard_total(cotangent, down_b), cross_shard_total(cotangent, down_b_dir)], axis=1).astype(jnp.bfloat16)
    gate_rank_rows = ranks[:, 0:R]
    up_rank_rows = ranks[:, R:2 * R]
    gate_rank_rows_direction = ranks[:, 2 * R:3 * R]
    up_rank_rows_direction = ranks[:, 3 * R:4 * R]
    adjoint_rank_rows = ranks[:, 4 * R:5 * R]
    adjoint_rank_rows_direction = ranks[:, 5 * R:6 * R]
    gate_preactivation = curvature_product(normed_tokens, gate_frozen_weight) + adapter_scale * curvature_product(gate_rank_rows, gate_output_factor)
    up_preactivation = curvature_product(normed_tokens, up_frozen_weight) + adapter_scale * curvature_product(up_rank_rows, up_output_factor)
    hidden_adjoint = cross_shard_total(cotangent, down_frozen_weight) + adapter_scale * cross_shard_total(adjoint_rank_rows, down_input_factor)
    gate_tangent_rows = adapter_scale * (curvature_product(gate_rank_rows_direction, gate_output_factor) + curvature_product(gate_rank_rows, gate_output_factor_direction))
    up_tangent_rows = adapter_scale * (curvature_product(up_rank_rows_direction, up_output_factor) + curvature_product(up_rank_rows, up_output_factor_direction))
    adjoint_tangent_rows = adapter_scale * (cross_shard_total(adjoint_rank_rows_direction, down_input_factor) + cross_shard_total(adjoint_rank_rows, down_input_factor_direction))
    hidden_activation, hidden_direction, gate_derivative, up_derivative, gate_derivative_direction, up_derivative_direction = second_order(gate_preactivation, up_preactivation, hidden_adjoint, gate_tangent_rows, up_tangent_rows, adjoint_tangent_rows)
    gate_quotient = cross_shard_total(gate_derivative, gate_output_factor)
    up_quotient = cross_shard_total(up_derivative, up_output_factor)
    gate_quotient_direction = cross_shard_total(gate_derivative_direction, gate_output_factor) + cross_shard_total(gate_derivative, gate_output_factor_direction)
    up_quotient_direction = cross_shard_total(up_derivative_direction, up_output_factor) + cross_shard_total(up_derivative, up_output_factor_direction)
    rank_direction = curvature_product(hidden_direction, down_input_factor) + curvature_product(hidden_activation, down_input_factor_direction)
    normed_feature_adjoint = cross_shard_total(gate_derivative, gate_frozen_weight) + cross_shard_total(up_derivative, up_frozen_weight) + adapter_scale * (exact_cross_total(gate_quotient, gate_input_factor) + exact_cross_total(up_quotient, up_input_factor))
    normed_feature_adjoint_direction = cross_shard_total(gate_derivative_direction, gate_frozen_weight) + cross_shard_total(up_derivative_direction, up_frozen_weight) + adapter_scale * (exact_cross_total(gate_quotient_direction, gate_input_factor) + exact_cross_total(gate_quotient, gate_input_factor_direction) + exact_cross_total(up_quotient_direction, up_input_factor) + exact_cross_total(up_quotient, up_input_factor_direction))
    curvature_gate_input = adapter_scale * exact_row_values(normed_tokens, gate_quotient_direction)
    curvature_up_input = adapter_scale * exact_row_values(normed_tokens, up_quotient_direction)
    curvature_gate_output = adapter_scale * (summed_over_rows(gate_rank_rows_direction, gate_derivative) + summed_over_rows(gate_rank_rows, gate_derivative_direction))
    curvature_up_output = adapter_scale * (summed_over_rows(up_rank_rows_direction, up_derivative) + summed_over_rows(up_rank_rows, up_derivative_direction))
    curvature_down_input = adapter_scale * (summed_over_rows(hidden_direction, adjoint_rank_rows) + summed_over_rows(hidden_activation, adjoint_rank_rows_direction))
    curvature_down_output = adapter_scale * exact_row_values(rank_direction, cotangent)
    return (normed_feature_adjoint, normed_feature_adjoint_direction, curvature_gate_input, curvature_gate_output, curvature_up_input, curvature_up_output, curvature_down_input, curvature_down_output)
```

```python
import functools

import jax
import jax.numpy as jnp
from jax import lax
from jax.experimental import pallas as pl
from jax.experimental.pallas import tpu as pltpu
from jax.sharding import PartitionSpec as P

adapter_scale = 0.5
epsilon = 1e-05
MESH = pl.DeviceIdType.MESH


def total_kernel(axis, n, x_ref, o_ref, inbox, whole, send1, recv1, send2, recv2):
    me = lax.axis_index(axis)
    barrier = pltpu.get_barrier_semaphore()

    @pl.loop(1, n)
    def _(k):
        pl.semaphore_signal(
            barrier, inc=1, device_id={axis: lax.rem(me + k, n)}, device_id_type=MESH
        )

    pl.semaphore_wait(barrier, n - 1)

    def scatter(k):
        peer = lax.rem(me + k, n)
        return pltpu.make_async_remote_copy(
            src_ref=x_ref.at[peer],
            dst_ref=inbox.at[k],
            send_sem=send1.at[k],
            recv_sem=recv1.at[k],
            device_id={axis: peer},
            device_id_type=MESH,
        )

    def spread(k):
        peer = lax.rem(me + k, n)
        return pltpu.make_async_remote_copy(
            src_ref=whole.at[me],
            dst_ref=whole.at[me],
            send_sem=send2.at[k],
            recv_sem=recv2.at[k],
            device_id={axis: peer},
            device_id_type=MESH,
        )

    def arrival(k):
        origin = lax.rem(me - k + n, n)
        return pltpu.make_async_remote_copy(
            src_ref=whole.at[origin],
            dst_ref=whole.at[origin],
            send_sem=send2.at[k],
            recv_sem=recv2.at[k],
            device_id={axis: origin},
            device_id_type=MESH,
        )

    @pl.loop(1, n)
    def _(k):
        scatter(k).start()

    def add(k, total):
        scatter(k).wait_recv()
        return total + inbox[k].astype(jnp.float32)

    total = lax.fori_loop(1, n, add, x_ref[me].astype(jnp.float32))
    whole[me] = total.astype(whole.dtype)

    @pl.loop(1, n)
    def _(k):
        spread(k).start()

    @pl.loop(1, n)
    def _(k):
        arrival(k).wait_recv()

    @pl.loop(1, n)
    def _(k):
        scatter(k).wait_send()
        spread(k).wait_send()

    o_ref[...] = whole[...]


def shard_total(x, axis, collective_id):
    n = lax.axis_size(axis)
    rows, columns = x.shape
    block = (n, rows // n, columns)
    total = pl.pallas_call(
        functools.partial(total_kernel, axis, n),
        out_shape=jax.ShapeDtypeStruct(block, jnp.bfloat16),
        in_specs=[pl.BlockSpec(memory_space=pltpu.VMEM)],
        out_specs=pl.BlockSpec(memory_space=pltpu.VMEM),
        scratch_shapes=[
            pltpu.VMEM(block, x.dtype),
            pltpu.VMEM(block, jnp.bfloat16),
            pltpu.SemaphoreType.DMA((n,)),
            pltpu.SemaphoreType.DMA((n,)),
            pltpu.SemaphoreType.DMA((n,)),
            pltpu.SemaphoreType.DMA((n,)),
        ],
        compiler_params=pltpu.CompilerParams(collective_id=collective_id, has_side_effects=True),
        name=f"total_{axis}",
    )(x.reshape(block))
    return total.reshape(rows, columns)


def curvature_product(left, right):
    return jnp.dot(left, right, preferred_element_type=jnp.float32)


def cross_shard_total(left, right):
    return lax.dot_general(
        left, right, (((1,), (1,)), ((), ())), preferred_element_type=jnp.float32
    )


def summed_over_rows(left, right):
    return lax.dot_general(
        left, right, (((0,), (0,)), ((), ())), preferred_element_type=jnp.float32
    )


def second_order(
    gate_preactivation,
    up_preactivation,
    hidden_adjoint,
    gate_tangent_rows,
    up_tangent_rows,
    adjoint_tangent_rows,
):
    sigma = jax.nn.sigmoid(gate_preactivation)
    silu_value = gate_preactivation * sigma
    slope = sigma * (1.0 + gate_preactivation * (1.0 - sigma))
    bend = sigma * (1.0 - sigma) * (2.0 + gate_preactivation * (1.0 - 2.0 * sigma))
    hidden_activation = (silu_value * up_preactivation).astype(jnp.bfloat16)
    hidden_direction = (
        slope * gate_tangent_rows * up_preactivation + silu_value * up_tangent_rows
    ).astype(jnp.bfloat16)
    gate_derivative = (hidden_adjoint * up_preactivation * slope).astype(jnp.bfloat16)
    up_derivative = (hidden_adjoint * silu_value).astype(jnp.bfloat16)
    gate_derivative_direction = (
        adjoint_tangent_rows * up_preactivation * slope
        + hidden_adjoint * (up_tangent_rows * slope + up_preactivation * bend * gate_tangent_rows)
    ).astype(jnp.bfloat16)
    up_derivative_direction = (
        adjoint_tangent_rows * silu_value + hidden_adjoint * slope * gate_tangent_rows
    ).astype(jnp.bfloat16)
    return (
        hidden_activation,
        hidden_direction,
        gate_derivative,
        up_derivative,
        gate_derivative_direction,
        up_derivative_direction,
    )


def chunk_count(width):
    for count in (4, 2):
        if width % (128 * count) == 0:
            return count
    return 1


def on_device(
    tokens,
    norm_gain,
    cotangent,
    gate_frozen_weight,
    up_frozen_weight,
    down_frozen_weight,
    gate_input_factor,
    gate_output_factor,
    up_input_factor,
    up_output_factor,
    down_input_factor,
    down_b,
    gate_input_factor_direction,
    gate_output_factor_direction,
    up_input_factor_direction,
    up_output_factor_direction,
    down_input_factor_direction,
    down_b_dir,
):
    rank = gate_input_factor.shape[1]
    width_rows, width_columns = gate_frozen_weight.shape
    features = width_rows * lax.axis_size("row")
    own_count = tokens.shape[0]
    cot_panel = lax.all_gather(cotangent, "col", axis=0, tiled=True)
    tokens_f = tokens.astype(jnp.float32)
    squares = lax.psum(jnp.sum(tokens_f * tokens_f, axis=1), "row")
    own_normed = (tokens_f * lax.rsqrt(squares[:, None] / features + epsilon) * norm_gain).astype(
        jnp.bfloat16
    )
    normed_tokens = lax.all_gather(own_normed, "col", axis=0, tiled=True)
    count = normed_tokens.shape[0]
    chunks = chunk_count(width_columns)
    wide = width_columns // chunks
    spans = [slice(index * wide, (index + 1) * wide) for index in range(chunks)]

    in_factors = jnp.concatenate(
        [
            gate_input_factor,
            up_input_factor,
            gate_input_factor_direction,
            up_input_factor_direction,
        ],
        axis=1,
    )
    out_factors = jnp.concatenate([down_b, down_b_dir], axis=0)

    summed_chunks = []
    for span in spans:
        partial = (
            curvature_product(normed_tokens, gate_frozen_weight[:, span]).astype(jnp.bfloat16),
            curvature_product(normed_tokens, up_frozen_weight[:, span]).astype(jnp.bfloat16),
            cross_shard_total(cot_panel, down_frozen_weight[span]).astype(jnp.bfloat16),
        )
        if summed_chunks:
            partial, summed_chunks[-1] = lax.optimization_barrier((partial, summed_chunks[-1]))
        summed_chunks.append(lax.psum(partial, "row"))

    projected = jnp.concatenate(
        [curvature_product(normed_tokens, in_factors), cross_shard_total(cot_panel, out_factors)],
        axis=1,
    )
    ranks = shard_total(projected, "row", 0)
    gate_low, up_low, gate_low_dir, up_low_dir, adj_low, adj_low_dir = [
        ranks[:, index * rank : (index + 1) * rank] for index in range(6)
    ]
    gate_pair = jnp.concatenate([gate_low_dir, gate_low], axis=1)
    up_pair = jnp.concatenate([up_low_dir, up_low], axis=1)
    adj_pair = jnp.concatenate([adj_low_dir, adj_low], axis=1)
    gate_stack = jnp.concatenate([gate_low_dir, gate_low], axis=0)
    up_stack = jnp.concatenate([up_low_dir, up_low], axis=0)
    adj_stack = jnp.concatenate([adj_low, adj_low_dir], axis=0)
    gate_out = jnp.concatenate([gate_output_factor, gate_output_factor_direction], axis=0)
    up_out = jnp.concatenate([up_output_factor, up_output_factor_direction], axis=0)
    down_in = jnp.concatenate([down_input_factor, down_input_factor_direction], axis=1)

    feature = 0.0
    gate_q = 0.0
    up_q = 0.0
    low_dir = 0.0
    gate_output, up_output, down_input = [], [], []
    for span, total in zip(spans, summed_chunks):
        gate_sum, up_sum, adj_sum = [value.astype(jnp.float32) for value in total]
        gate_pre = gate_sum + adapter_scale * curvature_product(
            gate_low, gate_output_factor[:, span]
        )
        up_pre = up_sum + adapter_scale * curvature_product(
            up_low, up_output_factor[:, span]
        )
        hidden_adj = adj_sum + adapter_scale * cross_shard_total(
            adj_low, down_input_factor[span]
        )
        gate_tan = adapter_scale * curvature_product(gate_pair, gate_out[:, span])
        up_tan = adapter_scale * curvature_product(up_pair, up_out[:, span])
        adj_tan = adapter_scale * cross_shard_total(adj_pair, down_in[span])
        hidden, hidden_dir, d_gate, d_up, d_gate_dir, d_up_dir = second_order(
            gate_pre, up_pre, hidden_adj, gate_tan, up_tan, adj_tan
        )
        gate_d = jnp.concatenate([d_gate, d_gate_dir], axis=0)
        up_d = jnp.concatenate([d_up, d_up_dir], axis=0)
        hidden_d = jnp.concatenate([hidden_dir, hidden], axis=0)
        gate_output.append(adapter_scale * summed_over_rows(gate_stack, gate_d))
        up_output.append(adapter_scale * summed_over_rows(up_stack, up_d))
        down_input.append(adapter_scale * summed_over_rows(hidden_d, adj_stack))
        gate_q = gate_q + cross_shard_total(gate_d, gate_out[:, span])
        up_q = up_q + cross_shard_total(up_d, up_out[:, span])
        low_dir = (
            low_dir
            + curvature_product(hidden_dir, down_input_factor[span])
            + curvature_product(hidden, down_input_factor_direction[span])
        )
        feature = (
            feature
            + cross_shard_total(gate_d, gate_frozen_weight[:, span])
            + cross_shard_total(up_d, up_frozen_weight[:, span])
        )

    summed = lax.psum_scatter(
        feature.astype(jnp.bfloat16).reshape(2, count, width_rows),
        "col",
        scatter_dimension=1,
        tiled=True,
    ).astype(jnp.float32)
    adjoints = shard_total(
        jnp.concatenate(
            [
                gate_q[:count, :rank],
                up_q[:count, :rank],
                gate_q[count:, :rank] + gate_q[:count, rank:],
                up_q[count:, :rank] + up_q[:count, rank:],
                low_dir,
            ],
            axis=1,
        ).astype(jnp.bfloat16),
        "col",
        1,
    )
    piece = lax.dynamic_slice_in_dim(adjoints, lax.axis_index("col") * own_count, own_count, 0)
    normed_feature_adjoint = summed[0] + adapter_scale * cross_shard_total(
        piece[:, : 2 * rank], in_factors[:, : 2 * rank]
    )
    normed_feature_adjoint_direction = summed[1] + adapter_scale * cross_shard_total(
        jnp.concatenate([piece[:, 2 * rank : 4 * rank], piece[:, : 2 * rank]], axis=1), in_factors
    )
    gate_input = adapter_scale * summed_over_rows(
        normed_tokens, adjoints[:, 2 * rank : 3 * rank]
    )
    up_input = adapter_scale * summed_over_rows(normed_tokens, adjoints[:, 3 * rank : 4 * rank])
    down_output = adapter_scale * summed_over_rows(adjoints[:, 4 * rank :], cot_panel)
    return (
        normed_feature_adjoint,
        normed_feature_adjoint_direction,
        gate_input,
        jnp.concatenate(gate_output, axis=1),
        up_input,
        jnp.concatenate(up_output, axis=1),
        jnp.concatenate(down_input, axis=0),
        down_output,
    )


def solution(mesh):
    in_specs = (
        P("col", "row"),
        P("row"),
        P("col", "row"),
        P("row", "col"),
        P("row", "col"),
        P("col", "row"),
        P("row", None),
        P(None, "col"),
        P("row", None),
        P(None, "col"),
        P("col", None),
        P(None, "row"),
        P("row", None),
        P(None, "col"),
        P("row", None),
        P(None, "col"),
        P("col", None),
        P(None, "row"),
    )
    out_specs = (
        P("col", "row"),
        P("col", "row"),
        P("row", None),
        P(None, "col"),
        P("row", None),
        P(None, "col"),
        P("col", None),
        P(None, "row"),
    )
    return jax.shard_map(
        on_device, mesh=mesh, in_specs=in_specs, out_specs=out_specs, check_vma=False
    )
```

```python
import functools

import jax
import jax.numpy as jnp
from jax import lax
from jax.experimental import pallas as pl
from jax.experimental.pallas import tpu as pltpu
from jax.sharding import PartitionSpec as P

adapter_scale = 0.5
epsilon = 1e-05
MESH = pl.DeviceIdType.MESH


def total_kernel(axis, n, x_ref, o_ref, inbox, whole, send1, recv1, send2, recv2):
    me = lax.axis_index(axis)
    barrier = pltpu.get_barrier_semaphore()

    @pl.loop(1, n)
    def _(k):
        pl.semaphore_signal(
            barrier, inc=1, device_id={axis: lax.rem(me + k, n)}, device_id_type=MESH
        )

    pl.semaphore_wait(barrier, n - 1)

    def scatter(k):
        peer = lax.rem(me + k, n)
        return pltpu.make_async_remote_copy(
            src_ref=x_ref.at[peer],
            dst_ref=inbox.at[k],
            send_sem=send1.at[k],
            recv_sem=recv1.at[k],
            device_id={axis: peer},
            device_id_type=MESH,
        )

    def spread(k):
        peer = lax.rem(me + k, n)
        return pltpu.make_async_remote_copy(
            src_ref=whole.at[me],
            dst_ref=whole.at[me],
            send_sem=send2.at[k],
            recv_sem=recv2.at[k],
            device_id={axis: peer},
            device_id_type=MESH,
        )

    def arrival(k):
        origin = lax.rem(me - k + n, n)
        return pltpu.make_async_remote_copy(
            src_ref=whole.at[origin],
            dst_ref=whole.at[origin],
            send_sem=send2.at[k],
            recv_sem=recv2.at[k],
            device_id={axis: origin},
            device_id_type=MESH,
        )

    @pl.loop(1, n)
    def _(k):
        scatter(k).start()

    def add(k, total):
        scatter(k).wait_recv()
        return total + inbox[k].astype(jnp.float32)

    total = lax.fori_loop(1, n, add, x_ref[me].astype(jnp.float32))
    whole[me] = total.astype(whole.dtype)

    @pl.loop(1, n)
    def _(k):
        spread(k).start()

    @pl.loop(1, n)
    def _(k):
        arrival(k).wait_recv()

    @pl.loop(1, n)
    def _(k):
        scatter(k).wait_send()
        spread(k).wait_send()

    o_ref[...] = whole[...]


def shard_total(x, axis, collective_id):
    n = lax.axis_size(axis)
    rows, columns = x.shape
    block = (n, rows // n, columns)
    total = pl.pallas_call(
        functools.partial(total_kernel, axis, n),
        out_shape=jax.ShapeDtypeStruct(block, jnp.bfloat16),
        in_specs=[pl.BlockSpec(memory_space=pltpu.VMEM)],
        out_specs=pl.BlockSpec(memory_space=pltpu.VMEM),
        scratch_shapes=[
            pltpu.VMEM(block, x.dtype),
            pltpu.VMEM(block, jnp.bfloat16),
            pltpu.SemaphoreType.DMA((n,)),
            pltpu.SemaphoreType.DMA((n,)),
            pltpu.SemaphoreType.DMA((n,)),
            pltpu.SemaphoreType.DMA((n,)),
        ],
        compiler_params=pltpu.CompilerParams(collective_id=collective_id, has_side_effects=True),
        name=f"total_{axis}",
    )(x.reshape(block))
    return total.reshape(rows, columns)


def curvature_product(left, right):
    return jnp.dot(left, right, preferred_element_type=jnp.float32)


def cross_shard_total(left, right):
    return lax.dot_general(
        left, right, (((1,), (1,)), ((), ())), preferred_element_type=jnp.float32
    )


def summed_over_rows(left, right):
    return lax.dot_general(
        left, right, (((0,), (0,)), ((), ())), preferred_element_type=jnp.float32
    )


def second_order(
    gate_preactivation,
    up_preactivation,
    hidden_adjoint,
    gate_tangent_rows,
    up_tangent_rows,
    adjoint_tangent_rows,
):
    sigma = jax.nn.sigmoid(gate_preactivation)
    silu_value = gate_preactivation * sigma
    slope = sigma * (1.0 + gate_preactivation * (1.0 - sigma))
    bend = sigma * (1.0 - sigma) * (2.0 + gate_preactivation * (1.0 - 2.0 * sigma))
    hidden_activation = (silu_value * up_preactivation).astype(jnp.bfloat16)
    hidden_direction = (
        slope * gate_tangent_rows * up_preactivation + silu_value * up_tangent_rows
    ).astype(jnp.bfloat16)
    gate_derivative = (hidden_adjoint * up_preactivation * slope).astype(jnp.bfloat16)
    up_derivative = (hidden_adjoint * silu_value).astype(jnp.bfloat16)
    gate_derivative_direction = (
        adjoint_tangent_rows * up_preactivation * slope
        + hidden_adjoint * (up_tangent_rows * slope + up_preactivation * bend * gate_tangent_rows)
    ).astype(jnp.bfloat16)
    up_derivative_direction = (
        adjoint_tangent_rows * silu_value + hidden_adjoint * slope * gate_tangent_rows
    ).astype(jnp.bfloat16)
    return (
        hidden_activation,
        hidden_direction,
        gate_derivative,
        up_derivative,
        gate_derivative_direction,
        up_derivative_direction,
    )


def block_kernel(
    x_ref,
    cot_ref,
    gate_hbm,
    up_hbm,
    down_hbm,
    gate_left,
    up_left,
    adj_left,
    gate_stack,
    up_stack,
    adj_stack,
    gate_out,
    up_out,
    down_in,
    feature_ref,
    gate_q,
    up_q,
    low_q,
    gate_curve,
    up_curve,
    down_curve,
    parts,
    first_in,
    second_out,
    second_in,
    whole,
    wide_buf,
    down_buf,
    total,
    send_sem,
    recv_sem,
    wide_sem,
    down_sem,
):
    me = lax.axis_index("row")
    flip_low = me + 1 - 2 * lax.rem(me, 2)
    flip_high = me + 2 - 4 * (me // 2)
    flip_both = 3 - me
    chunks, blocks, block, triple = parts.shape
    width = triple // 3
    count = x_ref.shape[0]
    depth = x_ref.shape[1]
    slots = wide_buf.shape[0]

    barrier = pltpu.get_barrier_semaphore()
    for peer in (flip_low, flip_high):
        pl.semaphore_signal(barrier, inc=1, device_id={"row": peer}, device_id_type=MESH)

    def lanes(c):
        return pl.ds(pl.multiple_of(c * width, width), width)

    def loads(c):
        slot, side = lax.rem(c, slots), lax.rem(c, 2)
        return [
            pltpu.make_async_copy(
                gate_hbm.at[:, lanes(c)], wide_buf.at[slot, 0], wide_sem.at[slot, 0]
            ),
            pltpu.make_async_copy(
                up_hbm.at[:, lanes(c)], wide_buf.at[slot, 1], wide_sem.at[slot, 1]
            ),
            pltpu.make_async_copy(down_hbm.at[lanes(c), :], down_buf.at[side], down_sem.at[side]),
        ]

    def send(src, dst, c, path, k, peer):
        return pltpu.make_async_remote_copy(
            src_ref=src,
            dst_ref=dst,
            send_sem=send_sem.at[c, path, k],
            recv_sem=recv_sem.at[c, path, k],
            device_id={"row": peer},
            device_id_type=MESH,
        )

    def ends(path):
        return (flip_low, flip_high) if path == 0 else (flip_high, flip_low)

    def sends(c, path, ks):
        near, far = ends(path)
        base = 4 * path
        table = [
            lambda: send(parts.at[c, base + near], first_in.at[c, path, 0], c, path, 0, near),
            lambda: send(parts.at[c, base + flip_both], first_in.at[c, path, 1], c, path, 1, near),
            lambda: send(second_out.at[c, path], second_in.at[c, path], c, path, 2, far),
            lambda: send(whole.at[c, base + me], whole.at[c, base + me], c, path, 3, far),
            lambda: send(whole.at[c, base + me], whole.at[c, base + me], c, path, 4, near),
            lambda: send(whole.at[c, base + far], whole.at[c, base + far], c, path, 5, near),
        ]
        return [table[k]() for k in ks]

    def arrivals(c, path, ks):
        near, far = ends(path)
        base = 4 * path
        table = [
            lambda: send(parts.at[c, base + me], first_in.at[c, path, 0], c, path, 0, near),
            lambda: send(parts.at[c, base + far], first_in.at[c, path, 1], c, path, 1, near),
            lambda: send(second_out.at[c, path], second_in.at[c, path], c, path, 2, far),
            lambda: send(whole.at[c, base + far], whole.at[c, base + far], c, path, 3, far),
            lambda: send(whole.at[c, base + near], whole.at[c, base + near], c, path, 4, near),
            lambda: send(whole.at[c, base + flip_both], whole.at[c, base + flip_both], c, path, 5, near),
        ]
        return [table[k]() for k in ks]

    def put(c, at, value):
        parts[c, :, :, at * width : (at + 1) * width] = value.astype(jnp.bfloat16).reshape(
            blocks, block, width
        )

    for copy in loads(0):
        copy.start()
    total[...] = jnp.zeros_like(total)
    gate_q[...] = jnp.zeros_like(gate_q)
    up_q[...] = jnp.zeros_like(up_q)
    low_q[...] = jnp.zeros_like(low_q)
    pl.semaphore_wait(barrier, 2)

    def project(c):
        for copy in loads(c):
            copy.wait()

        @pl.when(c + 1 < chunks)
        def _():
            for copy in loads(c + 1):
                copy.start()

        slot = lax.rem(c, slots)
        put(c, 0, curvature_product(x_ref[...], wide_buf[slot, 0]))
        put(c, 1, curvature_product(x_ref[...], wide_buf[slot, 1]))
        put(c, 2, cross_shard_total(cot_ref[...], down_buf[lax.rem(c, 2)]))
        for path in range(2):
            for copy in sends(c, path, (0, 1)):
                copy.start()

    def relay(c):
        for path in range(2):
            near, far = ends(path)
            for copy in arrivals(c, path, (0, 1)):
                copy.wait_recv()
            second_out[c, path] = (
                parts[c, 4 * path + far].astype(jnp.float32)
                + first_in[c, path, 1].astype(jnp.float32)
            ).astype(jnp.bfloat16)
            sends(c, path, (2,))[0].start()

    def settle(c):
        for path in range(2):
            arrivals(c, path, (2,))[0].wait_recv()
            whole[c, 4 * path + me] = (
                parts[c, 4 * path + me].astype(jnp.float32)
                + first_in[c, path, 0].astype(jnp.float32)
                + second_in[c, path].astype(jnp.float32)
            ).astype(jnp.bfloat16)
            for copy in sends(c, path, (3, 4)):
                copy.start()

    def forward(c):
        for path in range(2):
            arrivals(c, path, (3,))[0].wait_recv()
            sends(c, path, (5,))[0].start()

    def differentiate(c):
        for path in range(2):
            for copy in arrivals(c, path, (4, 5)):
                copy.wait_recv()

        def got(at):
            return (
                whole[c, :, :, at * width : (at + 1) * width]
                .reshape(count, width)
                .astype(jnp.float32)
            )

        gate_w, up_w, down_w = gate_out[:, lanes(c)], up_out[:, lanes(c)], down_in[lanes(c), :]
        gate_low = curvature_product(gate_left[...], gate_w)
        up_low = curvature_product(up_left[...], up_w)
        adj_low = cross_shard_total(adj_left[...], down_w)
        hidden, hidden_dir, d_gate, d_up, d_gate_dir, d_up_dir = second_order(
            got(0) + gate_low[:count],
            got(1) + up_low[:count],
            got(2) + adj_low[:count],
            gate_low[count:],
            up_low[count:],
            adj_low[count:],
        )
        gate_d = jnp.concatenate([d_gate, d_gate_dir], axis=0)
        up_d = jnp.concatenate([d_up, d_up_dir], axis=0)
        hidden_d = jnp.concatenate([hidden_dir, hidden], axis=0)
        gate_curve[:, lanes(c)] = curvature_product(gate_stack[...], gate_d)
        up_curve[:, lanes(c)] = curvature_product(up_stack[...], up_d)
        down_curve[:, lanes(c)] = curvature_product(adj_stack[...], hidden_d)
        gate_q[...] += cross_shard_total(gate_d, gate_w)
        up_q[...] += cross_shard_total(up_d, up_w)
        low_q[...] += curvature_product(hidden_d, down_w)
        slot = lax.rem(c, slots)
        piece = 512 if depth % 512 == 0 else depth
        for start in range(0, depth, piece):
            span = slice(start, start + piece)
            total[:, span] += cross_shard_total(
                gate_d, wide_buf[slot, 0, span, :]
            ) + cross_shard_total(up_d, wide_buf[slot, 1, span, :])

    @pl.loop(0, chunks + 4)
    def _(t):
        for lag, stage in enumerate((project, relay, settle, forward, differentiate)):

            @pl.when((t >= lag) & (t < chunks + lag))
            def _(lag=lag, stage=stage):
                stage(t - lag)

    @pl.loop(0, chunks)
    def _(c):
        for path in range(2):
            for copy in sends(c, path, range(6)):
                copy.wait_send()

    feature_ref[...] = total[...].astype(jnp.bfloat16)


def fused_block(x, cot, gate_w, up_w, down_w, ranks, gate_out, up_out, down_in, width):
    count, depth = x.shape
    columns = gate_w.shape[1]
    rank = ranks.shape[1] // 6
    chunks = columns // width
    half = ranks * adapter_scale
    gate, up, gate_dir, up_dir, adj, adj_dir = [
        half[:, index * rank : (index + 1) * rank] for index in range(6)
    ]
    empty = jnp.zeros_like(gate)

    def left(low, low_dir):
        return jnp.concatenate(
            [
                jnp.concatenate([low, empty], axis=1),
                jnp.concatenate([low_dir, low], axis=1),
            ],
            axis=0,
        )

    vmem = pl.BlockSpec(memory_space=pltpu.VMEM)
    anywhere = pl.BlockSpec(memory_space=pl.ANY)
    block = count // 8
    f32, bf16 = jnp.float32, jnp.bfloat16
    return pl.pallas_call(
        block_kernel,
        out_shape=[
            jax.ShapeDtypeStruct((2 * count, depth), bf16),
            jax.ShapeDtypeStruct((2 * count, 2 * rank), f32),
            jax.ShapeDtypeStruct((2 * count, 2 * rank), f32),
            jax.ShapeDtypeStruct((2 * count, 2 * rank), f32),
            jax.ShapeDtypeStruct((rank, columns), f32),
            jax.ShapeDtypeStruct((rank, columns), f32),
            jax.ShapeDtypeStruct((rank, columns), f32),
        ],
        in_specs=[vmem] * 2 + [anywhere] * 3 + [vmem] * 9,
        out_specs=[vmem] * 7,
        scratch_shapes=[
            pltpu.VMEM((chunks, 8, block, 3 * width), bf16),
            pltpu.VMEM((chunks, 2, 2, block, 3 * width), bf16),
            pltpu.VMEM((chunks, 2, block, 3 * width), bf16),
            pltpu.VMEM((chunks, 2, block, 3 * width), bf16),
            pltpu.VMEM((chunks, 8, block, 3 * width), bf16),
            pltpu.VMEM((6, 2, depth, width), bf16),
            pltpu.VMEM((2, width, depth), bf16),
            pltpu.VMEM((2 * count, depth), f32),
            pltpu.SemaphoreType.DMA((chunks, 2, 6)),
            pltpu.SemaphoreType.DMA((chunks, 2, 6)),
            pltpu.SemaphoreType.DMA((6, 2)),
            pltpu.SemaphoreType.DMA((2,)),
        ],
        compiler_params=pltpu.CompilerParams(
            collective_id=2, has_side_effects=True, vmem_limit_bytes=60 * 1024 * 1024
        ),
        name="block",
    )(
        x,
        cot,
        gate_w,
        up_w,
        down_w,
        left(gate, gate_dir),
        left(up, up_dir),
        left(adj, adj_dir),
        jnp.concatenate([gate_dir, gate], axis=0).T,
        jnp.concatenate([up_dir, up], axis=0).T,
        jnp.concatenate([adj, adj_dir], axis=0).T,
        gate_out,
        up_out,
        down_in,
    )


def chunk_count(width):
    for count in (4, 2):
        if width % (128 * count) == 0:
            return count
    return 1


def on_device(
    tokens,
    norm_gain,
    cotangent,
    gate_frozen_weight,
    up_frozen_weight,
    down_frozen_weight,
    gate_input_factor,
    gate_output_factor,
    up_input_factor,
    up_output_factor,
    down_input_factor,
    down_b,
    gate_input_factor_direction,
    gate_output_factor_direction,
    up_input_factor_direction,
    up_output_factor_direction,
    down_input_factor_direction,
    down_b_dir,
):
    rank = gate_input_factor.shape[1]
    width_rows, width_columns = gate_frozen_weight.shape
    features = width_rows * lax.axis_size("row")
    own_count = tokens.shape[0]
    cot_panel = lax.all_gather(cotangent, "col", axis=0, tiled=True)
    tokens_f = tokens.astype(jnp.float32)
    squares = lax.psum(jnp.sum(tokens_f * tokens_f, axis=1), "row")
    own_normed = (tokens_f * lax.rsqrt(squares[:, None] / features + epsilon) * norm_gain).astype(
        jnp.bfloat16
    )
    normed_tokens = lax.all_gather(own_normed, "col", axis=0, tiled=True)
    count = normed_tokens.shape[0]
    in_factors = jnp.concatenate(
        [
            gate_input_factor,
            up_input_factor,
            gate_input_factor_direction,
            up_input_factor_direction,
        ],
        axis=1,
    )
    out_factors = jnp.concatenate([down_b, down_b_dir], axis=0)

    projected = jnp.concatenate(
        [curvature_product(normed_tokens, in_factors), cross_shard_total(cot_panel, out_factors)],
        axis=1,
    )
    ranks = shard_total(projected, "row", 0)
    gate_out = jnp.concatenate([gate_output_factor, gate_output_factor_direction], axis=0)
    up_out = jnp.concatenate([up_output_factor, up_output_factor_direction], axis=0)
    down_in = jnp.concatenate([down_input_factor, down_input_factor_direction], axis=1)

    width = 256
    if lax.axis_size("row") == 4 and width_columns % width == 0 and count % 128 == 0:
        feature, gate_q, up_q, low_q, gate_output, up_output, down_input = fused_block(
            normed_tokens,
            cot_panel,
            gate_frozen_weight,
            up_frozen_weight,
            down_frozen_weight,
            ranks,
            gate_out,
            up_out,
            down_in,
            width,
        )
        low_dir = low_q[:count, :rank] + low_q[count:, rank:]
        down_input = down_input.T
    else:
        chunks = chunk_count(width_columns)
        wide = width_columns // chunks
        spans = [slice(index * wide, (index + 1) * wide) for index in range(chunks)]

        summed_chunks = []
        for span in spans:
            partial = (
                curvature_product(normed_tokens, gate_frozen_weight[:, span]).astype(jnp.bfloat16),
                curvature_product(normed_tokens, up_frozen_weight[:, span]).astype(jnp.bfloat16),
                cross_shard_total(cot_panel, down_frozen_weight[span]).astype(jnp.bfloat16),
            )
            if summed_chunks:
                partial, summed_chunks[-1] = lax.optimization_barrier((partial, summed_chunks[-1]))
            summed_chunks.append(lax.psum(partial, "row"))

        gate_low, up_low, gate_low_dir, up_low_dir, adj_low, adj_low_dir = [
            ranks[:, index * rank : (index + 1) * rank] for index in range(6)
        ]
        gate_pair = jnp.concatenate([gate_low_dir, gate_low], axis=1)
        up_pair = jnp.concatenate([up_low_dir, up_low], axis=1)
        adj_pair = jnp.concatenate([adj_low_dir, adj_low], axis=1)
        gate_stack = jnp.concatenate([gate_low_dir, gate_low], axis=0)
        up_stack = jnp.concatenate([up_low_dir, up_low], axis=0)
        adj_stack = jnp.concatenate([adj_low, adj_low_dir], axis=0)
        feature = 0.0
        gate_q = 0.0
        up_q = 0.0
        low_dir = 0.0
        gate_output, up_output, down_input = [], [], []
        for span, total in zip(spans, summed_chunks):
            gate_sum, up_sum, adj_sum = [value.astype(jnp.float32) for value in total]
            gate_pre = gate_sum + adapter_scale * curvature_product(
                gate_low, gate_output_factor[:, span]
            )
            up_pre = up_sum + adapter_scale * curvature_product(
                up_low, up_output_factor[:, span]
            )
            hidden_adj = adj_sum + adapter_scale * cross_shard_total(
                adj_low, down_input_factor[span]
            )
            gate_tan = adapter_scale * curvature_product(gate_pair, gate_out[:, span])
            up_tan = adapter_scale * curvature_product(up_pair, up_out[:, span])
            adj_tan = adapter_scale * cross_shard_total(adj_pair, down_in[span])
            hidden, hidden_dir, d_gate, d_up, d_gate_dir, d_up_dir = second_order(
                gate_pre, up_pre, hidden_adj, gate_tan, up_tan, adj_tan
            )
            gate_d = jnp.concatenate([d_gate, d_gate_dir], axis=0)
            up_d = jnp.concatenate([d_up, d_up_dir], axis=0)
            hidden_d = jnp.concatenate([hidden_dir, hidden], axis=0)
            gate_output.append(adapter_scale * summed_over_rows(gate_stack, gate_d))
            up_output.append(adapter_scale * summed_over_rows(up_stack, up_d))
            down_input.append(adapter_scale * summed_over_rows(hidden_d, adj_stack))
            gate_q = gate_q + cross_shard_total(gate_d, gate_out[:, span])
            up_q = up_q + cross_shard_total(up_d, up_out[:, span])
            low_dir = (
                low_dir
                + curvature_product(hidden_dir, down_input_factor[span])
                + curvature_product(hidden, down_input_factor_direction[span])
            )
            feature = (
                feature
                + cross_shard_total(gate_d, gate_frozen_weight[:, span])
                + cross_shard_total(up_d, up_frozen_weight[:, span])
            )
        gate_output = jnp.concatenate(gate_output, axis=1)
        up_output = jnp.concatenate(up_output, axis=1)
        down_input = jnp.concatenate(down_input, axis=0)

    summed = lax.psum_scatter(
        feature.astype(jnp.bfloat16).reshape(2, count, width_rows),
        "col",
        scatter_dimension=1,
        tiled=True,
    ).astype(jnp.float32)
    adjoints = shard_total(
        jnp.concatenate(
            [
                gate_q[:count, :rank],
                up_q[:count, :rank],
                gate_q[count:, :rank] + gate_q[:count, rank:],
                up_q[count:, :rank] + up_q[:count, rank:],
                low_dir,
            ],
            axis=1,
        ).astype(jnp.bfloat16),
        "col",
        1,
    )
    piece = lax.dynamic_slice_in_dim(adjoints, lax.axis_index("col") * own_count, own_count, 0)
    normed_feature_adjoint = summed[0] + adapter_scale * cross_shard_total(
        piece[:, : 2 * rank], in_factors[:, : 2 * rank]
    )
    normed_feature_adjoint_direction = summed[1] + adapter_scale * cross_shard_total(
        jnp.concatenate([piece[:, 2 * rank : 4 * rank], piece[:, : 2 * rank]], axis=1), in_factors
    )
    gate_input = adapter_scale * summed_over_rows(
        normed_tokens, adjoints[:, 2 * rank : 3 * rank]
    )
    up_input = adapter_scale * summed_over_rows(normed_tokens, adjoints[:, 3 * rank : 4 * rank])
    down_output = adapter_scale * summed_over_rows(adjoints[:, 4 * rank :], cot_panel)
    return (
        normed_feature_adjoint,
        normed_feature_adjoint_direction,
        gate_input,
        gate_output,
        up_input,
        up_output,
        down_input,
        down_output,
    )


def solution(mesh):
    in_specs = (
        P("col", "row"),
        P("row"),
        P("col", "row"),
        P("row", "col"),
        P("row", "col"),
        P("col", "row"),
        P("row", None),
        P(None, "col"),
        P("row", None),
        P(None, "col"),
        P("col", None),
        P(None, "row"),
        P("row", None),
        P(None, "col"),
        P("row", None),
        P(None, "col"),
        P("col", None),
        P(None, "row"),
    )
    out_specs = (
        P("col", "row"),
        P("col", "row"),
        P("row", None),
        P(None, "col"),
        P("row", None),
        P(None, "col"),
        P("col", None),
        P(None, "row"),
    )
    return jax.shard_map(
        on_device, mesh=mesh, in_specs=in_specs, out_specs=out_specs, check_vma=False
    )
```

```python
import functools

import jax
import jax.numpy as jnp
from jax import lax
from jax.experimental import pallas as pl
from jax.experimental.pallas import tpu as pltpu
from jax.sharding import PartitionSpec as P

adapter_scale = 0.5
epsilon = 1e-05
MESH = pl.DeviceIdType.MESH


def total_kernel(axis, n, x_ref, o_ref, inbox, whole, send1, recv1, send2, recv2):
    me = lax.axis_index(axis)
    barrier = pltpu.get_barrier_semaphore()

    @pl.loop(1, n)
    def _(k):
        pl.semaphore_signal(
            barrier, inc=1, device_id={axis: lax.rem(me + k, n)}, device_id_type=MESH
        )

    pl.semaphore_wait(barrier, n - 1)

    def scatter(k):
        peer = lax.rem(me + k, n)
        return pltpu.make_async_remote_copy(
            src_ref=x_ref.at[peer],
            dst_ref=inbox.at[k],
            send_sem=send1.at[k],
            recv_sem=recv1.at[k],
            device_id={axis: peer},
            device_id_type=MESH,
        )

    def spread(k):
        peer = lax.rem(me + k, n)
        return pltpu.make_async_remote_copy(
            src_ref=whole.at[me],
            dst_ref=whole.at[me],
            send_sem=send2.at[k],
            recv_sem=recv2.at[k],
            device_id={axis: peer},
            device_id_type=MESH,
        )

    def arrival(k):
        origin = lax.rem(me - k + n, n)
        return pltpu.make_async_remote_copy(
            src_ref=whole.at[origin],
            dst_ref=whole.at[origin],
            send_sem=send2.at[k],
            recv_sem=recv2.at[k],
            device_id={axis: origin},
            device_id_type=MESH,
        )

    @pl.loop(1, n)
    def _(k):
        scatter(k).start()

    def add(k, total):
        scatter(k).wait_recv()
        return total + inbox[k].astype(jnp.float32)

    total = lax.fori_loop(1, n, add, x_ref[me].astype(jnp.float32))
    whole[me] = total.astype(whole.dtype)

    @pl.loop(1, n)
    def _(k):
        spread(k).start()

    @pl.loop(1, n)
    def _(k):
        arrival(k).wait_recv()

    @pl.loop(1, n)
    def _(k):
        scatter(k).wait_send()
        spread(k).wait_send()

    o_ref[...] = whole[...]


def shard_total(x, axis, collective_id):
    n = lax.axis_size(axis)
    rows, columns = x.shape
    block = (n, rows // n, columns)
    total = pl.pallas_call(
        functools.partial(total_kernel, axis, n),
        out_shape=jax.ShapeDtypeStruct(block, jnp.bfloat16),
        in_specs=[pl.BlockSpec(memory_space=pltpu.VMEM)],
        out_specs=pl.BlockSpec(memory_space=pltpu.VMEM),
        scratch_shapes=[
            pltpu.VMEM(block, x.dtype),
            pltpu.VMEM(block, jnp.bfloat16),
            pltpu.SemaphoreType.DMA((n,)),
            pltpu.SemaphoreType.DMA((n,)),
            pltpu.SemaphoreType.DMA((n,)),
            pltpu.SemaphoreType.DMA((n,)),
        ],
        compiler_params=pltpu.CompilerParams(collective_id=collective_id, has_side_effects=True),
        name=f"total_{axis}",
    )(x.reshape(block))
    return total.reshape(rows, columns)


def curvature_product(left, right):
    return jnp.dot(left, right, preferred_element_type=jnp.float32)


def cross_shard_total(left, right):
    return lax.dot_general(
        left, right, (((1,), (1,)), ((), ())), preferred_element_type=jnp.float32
    )


def summed_over_rows(left, right):
    return lax.dot_general(
        left, right, (((0,), (0,)), ((), ())), preferred_element_type=jnp.float32
    )


def second_order(
    gate_preactivation,
    up_preactivation,
    hidden_adjoint,
    gate_tangent_rows,
    up_tangent_rows,
    adjoint_tangent_rows,
):
    sigma = jax.nn.sigmoid(gate_preactivation)
    silu_value = gate_preactivation * sigma
    slope = sigma * (1.0 + gate_preactivation * (1.0 - sigma))
    bend = sigma * (1.0 - sigma) * (2.0 + gate_preactivation * (1.0 - 2.0 * sigma))
    hidden_activation = (silu_value * up_preactivation).astype(jnp.bfloat16)
    hidden_direction = (
        slope * gate_tangent_rows * up_preactivation + silu_value * up_tangent_rows
    ).astype(jnp.bfloat16)
    gate_derivative = (hidden_adjoint * up_preactivation * slope).astype(jnp.bfloat16)
    up_derivative = (hidden_adjoint * silu_value).astype(jnp.bfloat16)
    gate_derivative_direction = (
        adjoint_tangent_rows * up_preactivation * slope
        + hidden_adjoint * (up_tangent_rows * slope + up_preactivation * bend * gate_tangent_rows)
    ).astype(jnp.bfloat16)
    up_derivative_direction = (
        adjoint_tangent_rows * silu_value + hidden_adjoint * slope * gate_tangent_rows
    ).astype(jnp.bfloat16)
    return (
        hidden_activation,
        hidden_direction,
        gate_derivative,
        up_derivative,
        gate_derivative_direction,
        up_derivative_direction,
    )


def block_kernel(
    x_ref,
    cot_ref,
    gate_hbm,
    up_hbm,
    down_hbm,
    gate_left,
    up_left,
    adj_left,
    gate_stack,
    up_stack,
    adj_stack,
    gate_out,
    up_out,
    down_in,
    feature_ref,
    gate_q,
    up_q,
    low_q,
    gate_curve,
    up_curve,
    down_curve,
    parts,
    first_in,
    second_out,
    second_in,
    whole,
    wide_buf,
    down_buf,
    total,
    send_sem,
    recv_sem,
    wide_sem,
    down_sem,
):
    me = lax.axis_index("row")
    flip_low = me + 1 - 2 * lax.rem(me, 2)
    flip_high = me + 2 - 4 * (me // 2)
    flip_both = 3 - me
    chunks, blocks, block, triple = parts.shape
    width = triple // 3
    count = x_ref.shape[0]
    depth = x_ref.shape[1]
    slots = wide_buf.shape[0]

    barrier = pltpu.get_barrier_semaphore()
    for peer in (flip_low, flip_high):
        pl.semaphore_signal(barrier, inc=1, device_id={"row": peer}, device_id_type=MESH)

    def lanes(c):
        return pl.ds(pl.multiple_of(c * width, width), width)

    def loads(c):
        slot, side = lax.rem(c, slots), lax.rem(c, 2)
        return [
            pltpu.make_async_copy(
                gate_hbm.at[:, lanes(c)], wide_buf.at[slot, 0], wide_sem.at[slot, 0]
            ),
            pltpu.make_async_copy(
                up_hbm.at[:, lanes(c)], wide_buf.at[slot, 1], wide_sem.at[slot, 1]
            ),
            pltpu.make_async_copy(down_hbm.at[lanes(c), :], down_buf.at[side], down_sem.at[side]),
        ]

    def send(src, dst, c, path, k, peer):
        return pltpu.make_async_remote_copy(
            src_ref=src,
            dst_ref=dst,
            send_sem=send_sem.at[c, path, k],
            recv_sem=recv_sem.at[c, path, k],
            device_id={"row": peer},
            device_id_type=MESH,
        )

    def ends(path):
        return (flip_low, flip_high) if path == 0 else (flip_high, flip_low)

    def sends(c, path, ks):
        near, far = ends(path)
        base = 4 * path
        table = [
            lambda: send(parts.at[c, base + near], first_in.at[c, path, 0], c, path, 0, near),
            lambda: send(parts.at[c, base + flip_both], first_in.at[c, path, 1], c, path, 1, near),
            lambda: send(second_out.at[c, path], second_in.at[c, path], c, path, 2, far),
            lambda: send(whole.at[c, base + me], whole.at[c, base + me], c, path, 3, far),
            lambda: send(whole.at[c, base + me], whole.at[c, base + me], c, path, 4, near),
            lambda: send(whole.at[c, base + far], whole.at[c, base + far], c, path, 5, near),
        ]
        return [table[k]() for k in ks]

    def arrivals(c, path, ks):
        near, far = ends(path)
        base = 4 * path
        table = [
            lambda: send(parts.at[c, base + me], first_in.at[c, path, 0], c, path, 0, near),
            lambda: send(parts.at[c, base + far], first_in.at[c, path, 1], c, path, 1, near),
            lambda: send(second_out.at[c, path], second_in.at[c, path], c, path, 2, far),
            lambda: send(whole.at[c, base + far], whole.at[c, base + far], c, path, 3, far),
            lambda: send(whole.at[c, base + near], whole.at[c, base + near], c, path, 4, near),
            lambda: send(whole.at[c, base + flip_both], whole.at[c, base + flip_both], c, path, 5, near),
        ]
        return [table[k]() for k in ks]

    def put(c, at, value):
        parts[c, :, :, at * width : (at + 1) * width] = value.astype(jnp.bfloat16).reshape(
            blocks, block, width
        )

    for copy in loads(0):
        copy.start()
    total[...] = jnp.zeros_like(total)
    gate_q[...] = jnp.zeros_like(gate_q)
    up_q[...] = jnp.zeros_like(up_q)
    low_q[...] = jnp.zeros_like(low_q)
    pl.semaphore_wait(barrier, 2)

    def project(c):
        for copy in loads(c):
            copy.wait()

        @pl.when(c + 1 < chunks)
        def _():
            for copy in loads(c + 1):
                copy.start()

        slot = lax.rem(c, slots)
        put(c, 0, curvature_product(x_ref[...], wide_buf[slot, 0]))
        put(c, 1, curvature_product(x_ref[...], wide_buf[slot, 1]))
        put(c, 2, cross_shard_total(cot_ref[...], down_buf[lax.rem(c, 2)]))
        for path in range(2):
            for copy in sends(c, path, (0, 1)):
                copy.start()

    def relay(c):
        for path in range(2):
            near, far = ends(path)
            for copy in arrivals(c, path, (0, 1)):
                copy.wait_recv()
            second_out[c, path] = (
                parts[c, 4 * path + far].astype(jnp.float32)
                + first_in[c, path, 1].astype(jnp.float32)
            ).astype(jnp.bfloat16)
            sends(c, path, (2,))[0].start()

    def settle(c):
        for path in range(2):
            arrivals(c, path, (2,))[0].wait_recv()
            whole[c, 4 * path + me] = (
                parts[c, 4 * path + me].astype(jnp.float32)
                + first_in[c, path, 0].astype(jnp.float32)
                + second_in[c, path].astype(jnp.float32)
            ).astype(jnp.bfloat16)
            for copy in sends(c, path, (3, 4)):
                copy.start()

    def forward(c):
        for path in range(2):
            arrivals(c, path, (3,))[0].wait_recv()
            sends(c, path, (5,))[0].start()

    def differentiate(c):
        for path in range(2):
            for copy in arrivals(c, path, (4, 5)):
                copy.wait_recv()

        def got(at):
            return (
                whole[c, :, :, at * width : (at + 1) * width]
                .reshape(count, width)
                .astype(jnp.float32)
            )

        gate_w, up_w, down_w = gate_out[:, lanes(c)], up_out[:, lanes(c)], down_in[lanes(c), :]
        gate_low = curvature_product(gate_left[...], gate_w)
        up_low = curvature_product(up_left[...], up_w)
        adj_low = cross_shard_total(adj_left[...], down_w)
        hidden, hidden_dir, d_gate, d_up, d_gate_dir, d_up_dir = second_order(
            got(0) + gate_low[:count],
            got(1) + up_low[:count],
            got(2) + adj_low[:count],
            gate_low[count:],
            up_low[count:],
            adj_low[count:],
        )
        gate_d = jnp.concatenate([d_gate, d_gate_dir], axis=0)
        up_d = jnp.concatenate([d_up, d_up_dir], axis=0)
        hidden_d = jnp.concatenate([hidden_dir, hidden], axis=0)
        gate_curve[:, lanes(c)] = curvature_product(gate_stack[...], gate_d)
        up_curve[:, lanes(c)] = curvature_product(up_stack[...], up_d)
        down_curve[:, lanes(c)] = curvature_product(adj_stack[...], hidden_d)
        gate_q[...] += cross_shard_total(gate_d, gate_w)
        up_q[...] += cross_shard_total(up_d, up_w)
        low_q[...] += curvature_product(hidden_d, down_w)
        slot = lax.rem(c, slots)
        piece = 512 if depth % 512 == 0 else depth
        for start in range(0, depth, piece):
            span = slice(start, start + piece)
            total[:, span] += cross_shard_total(
                gate_d, wide_buf[slot, 0, span, :]
            ) + cross_shard_total(up_d, wide_buf[slot, 1, span, :])

    @pl.loop(0, chunks + 4)
    def _(t):
        for lag, stage in enumerate((project, relay, settle, forward, differentiate)):

            @pl.when((t >= lag) & (t < chunks + lag))
            def _(lag=lag, stage=stage):
                stage(t - lag)

    @pl.loop(0, chunks)
    def _(c):
        for path in range(2):
            for copy in sends(c, path, range(6)):
                copy.wait_send()

    feature_ref[...] = total[...].astype(jnp.bfloat16)


def fused_block(x, cot, gate_w, up_w, down_w, ranks, gate_out, up_out, down_in, width):
    count, depth = x.shape
    columns = gate_w.shape[1]
    rank = ranks.shape[1] // 6
    chunks = columns // width
    half = ranks * adapter_scale
    gate, up, gate_dir, up_dir, adj, adj_dir = [
        half[:, index * rank : (index + 1) * rank] for index in range(6)
    ]
    empty = jnp.zeros_like(gate)

    def left(low, low_dir):
        return jnp.concatenate(
            [
                jnp.concatenate([low, empty], axis=1),
                jnp.concatenate([low_dir, low], axis=1),
            ],
            axis=0,
        )

    vmem = pl.BlockSpec(memory_space=pltpu.VMEM)
    anywhere = pl.BlockSpec(memory_space=pl.ANY)
    block = count // 8
    f32, bf16 = jnp.float32, jnp.bfloat16
    return pl.pallas_call(
        block_kernel,
        out_shape=[
            jax.ShapeDtypeStruct((2 * count, depth), bf16),
            jax.ShapeDtypeStruct((2 * count, 2 * rank), f32),
            jax.ShapeDtypeStruct((2 * count, 2 * rank), f32),
            jax.ShapeDtypeStruct((2 * count, 2 * rank), f32),
            jax.ShapeDtypeStruct((rank, columns), f32),
            jax.ShapeDtypeStruct((rank, columns), f32),
            jax.ShapeDtypeStruct((rank, columns), f32),
        ],
        in_specs=[vmem] * 2 + [anywhere] * 3 + [vmem] * 9,
        out_specs=[vmem] * 7,
        scratch_shapes=[
            pltpu.VMEM((chunks, 8, block, 3 * width), bf16),
            pltpu.VMEM((chunks, 2, 2, block, 3 * width), bf16),
            pltpu.VMEM((chunks, 2, block, 3 * width), bf16),
            pltpu.VMEM((chunks, 2, block, 3 * width), bf16),
            pltpu.VMEM((chunks, 8, block, 3 * width), bf16),
            pltpu.VMEM((6, 2, depth, width), bf16),
            pltpu.VMEM((2, width, depth), bf16),
            pltpu.VMEM((2 * count, depth), f32),
            pltpu.SemaphoreType.DMA((chunks, 2, 6)),
            pltpu.SemaphoreType.DMA((chunks, 2, 6)),
            pltpu.SemaphoreType.DMA((6, 2)),
            pltpu.SemaphoreType.DMA((2,)),
        ],
        compiler_params=pltpu.CompilerParams(
            collective_id=2, has_side_effects=True, vmem_limit_bytes=60 * 1024 * 1024
        ),
        name="block",
    )(
        x,
        cot,
        gate_w,
        up_w,
        down_w,
        left(gate, gate_dir),
        left(up, up_dir),
        left(adj, adj_dir),
        jnp.concatenate([gate_dir, gate], axis=0).T,
        jnp.concatenate([up_dir, up], axis=0).T,
        jnp.concatenate([adj, adj_dir], axis=0).T,
        gate_out,
        up_out,
        down_in,
    )


def gather_kernel(
    tokens,
    gain,
    cot,
    x_all,
    cot_all,
    x_buf,
    cot_buf,
    squares,
    square_send,
    square_recv,
    far_send,
    far_recv,
    near_send,
    near_recv,
):
    rows, columns = lax.axis_size("row"), lax.axis_size("col")
    chips = columns // 2
    my_row, me = lax.axis_index("row"), lax.axis_index("col")
    partner = me + 1 - 2 * lax.rem(me, 2)
    features = rows * tokens.shape[1]
    barrier = pltpu.get_barrier_semaphore()

    def row_peer(k):
        return {"row": lax.rem(my_row + k, rows)}

    def far_peer(k):
        return {"col": lax.rem(me + 2 * k, columns)}

    @pl.loop(1, rows)
    def _(k):
        pl.semaphore_signal(barrier, inc=1, device_id=row_peer(k), device_id_type=MESH)

    @pl.loop(1, chips)
    def _(k):
        pl.semaphore_signal(barrier, inc=1, device_id=far_peer(k), device_id_type=MESH)

    pl.semaphore_signal(barrier, inc=1, device_id={"col": partner}, device_id_type=MESH)

    buffers = (cot_buf, x_buf)

    def origin(k):
        return lax.rem(me - 2 * k + columns, columns)

    def square(k):
        return pltpu.make_async_remote_copy(
            src_ref=squares.at[0],
            dst_ref=squares.at[k],
            send_sem=square_send.at[k],
            recv_sem=square_recv.at[k],
            device_id=row_peer(k),
            device_id_type=MESH,
        )

    def far(which, k, slot):
        return pltpu.make_async_remote_copy(
            src_ref=buffers[which].at[slot],
            dst_ref=buffers[which].at[slot],
            send_sem=far_send.at[which, k],
            recv_sem=far_recv.at[which, k],
            device_id=far_peer(k),
            device_id_type=MESH,
        )

    def near(which, k, slot):
        return pltpu.make_async_remote_copy(
            src_ref=buffers[which].at[slot],
            dst_ref=buffers[which].at[slot],
            send_sem=near_send.at[which, k],
            recv_sem=near_recv.at[which, k],
            device_id={"col": partner},
            device_id_type=MESH,
        )

    def launch(which):
        @pl.loop(1, chips)
        def _(k):
            far(which, k, me).start()

        near(which, 0, me).start()

    values = tokens[...].astype(jnp.float32)
    squares[0] = jnp.broadcast_to(
        jnp.sum(values * values, axis=1, keepdims=True), squares.shape[1:]
    )
    cot_buf[me] = cot[...]
    pl.semaphore_wait(barrier, rows + chips - 1)

    @pl.loop(1, rows)
    def _(k):
        square(k).start()

    launch(0)

    def add(k, total):
        square(k).wait_recv()
        return total + squares[k]

    total = lax.fori_loop(1, rows, add, squares[0])
    scale = lax.rsqrt(total[:, :1] / features + epsilon)
    x_buf[me] = (tokens[...].astype(jnp.float32) * scale * gain[...]).astype(jnp.bfloat16)
    launch(1)
    for which in range(2):

        @pl.loop(1, chips)
        def _(k, which=which):
            far(which, k, origin(k)).wait_recv()
            near(which, k, origin(k)).start()

    for which in range(2):

        @pl.loop(0, chips)
        def _(k, which=which):
            near(which, k, lax.rem(partner - 2 * k + columns, columns)).wait_recv()

    @pl.loop(1, rows)
    def _(k):
        square(k).wait_send()

    for which in range(2):

        @pl.loop(1, chips)
        def _(k, which=which):
            far(which, k, me).wait_send()

        @pl.loop(0, chips)
        def _(k, which=which):
            near(which, k, origin(k)).wait_send()

    cot_all[...] = cot_buf[...]
    x_all[...] = x_buf[...]


def gathered(tokens, gain, cot):
    rows, columns = lax.axis_size("row"), lax.axis_size("col")
    own, depth = tokens.shape
    whole = (columns, own, depth)
    vmem = pl.BlockSpec(memory_space=pltpu.VMEM)
    x, panel = pl.pallas_call(
        gather_kernel,
        out_shape=[jax.ShapeDtypeStruct(whole, jnp.bfloat16)] * 2,
        in_specs=[vmem] * 3,
        out_specs=[vmem] * 2,
        scratch_shapes=[
            pltpu.VMEM(whole, jnp.bfloat16),
            pltpu.VMEM(whole, jnp.bfloat16),
            pltpu.VMEM((rows, own, 128), jnp.float32),
            pltpu.SemaphoreType.DMA((rows,)),
            pltpu.SemaphoreType.DMA((rows,)),
            pltpu.SemaphoreType.DMA((2, columns // 2)),
            pltpu.SemaphoreType.DMA((2, columns // 2)),
            pltpu.SemaphoreType.DMA((2, columns // 2)),
            pltpu.SemaphoreType.DMA((2, columns // 2)),
        ],
        compiler_params=pltpu.CompilerParams(collective_id=3, has_side_effects=True),
        name="gather",
    )(tokens, gain.reshape(1, depth), cot)
    return x.reshape(columns * own, depth), panel.reshape(columns * own, depth)


def chunk_count(width):
    for count in (4, 2):
        if width % (128 * count) == 0:
            return count
    return 1


def on_device(
    tokens,
    norm_gain,
    cotangent,
    gate_frozen_weight,
    up_frozen_weight,
    down_frozen_weight,
    gate_input_factor,
    gate_output_factor,
    up_input_factor,
    up_output_factor,
    down_input_factor,
    down_b,
    gate_input_factor_direction,
    gate_output_factor_direction,
    up_input_factor_direction,
    up_output_factor_direction,
    down_input_factor_direction,
    down_b_dir,
):
    rank = gate_input_factor.shape[1]
    width_rows, width_columns = gate_frozen_weight.shape
    own_count = tokens.shape[0]
    normed_tokens, cot_panel = gathered(tokens, norm_gain, cotangent)
    count = normed_tokens.shape[0]
    in_factors = jnp.concatenate(
        [
            gate_input_factor,
            up_input_factor,
            gate_input_factor_direction,
            up_input_factor_direction,
        ],
        axis=1,
    )
    out_factors = jnp.concatenate([down_b, down_b_dir], axis=0)

    projected = jnp.concatenate(
        [curvature_product(normed_tokens, in_factors), cross_shard_total(cot_panel, out_factors)],
        axis=1,
    )
    ranks = shard_total(projected, "row", 0)
    gate_out = jnp.concatenate([gate_output_factor, gate_output_factor_direction], axis=0)
    up_out = jnp.concatenate([up_output_factor, up_output_factor_direction], axis=0)
    down_in = jnp.concatenate([down_input_factor, down_input_factor_direction], axis=1)

    width = 256
    if lax.axis_size("row") == 4 and width_columns % width == 0 and count % 128 == 0:
        feature, gate_q, up_q, low_q, gate_output, up_output, down_input = fused_block(
            normed_tokens,
            cot_panel,
            gate_frozen_weight,
            up_frozen_weight,
            down_frozen_weight,
            ranks,
            gate_out,
            up_out,
            down_in,
            width,
        )
        low_dir = low_q[:count, :rank] + low_q[count:, rank:]
        down_input = down_input.T
    else:
        chunks = chunk_count(width_columns)
        wide = width_columns // chunks
        spans = [slice(index * wide, (index + 1) * wide) for index in range(chunks)]

        summed_chunks = []
        for span in spans:
            partial = (
                curvature_product(normed_tokens, gate_frozen_weight[:, span]).astype(jnp.bfloat16),
                curvature_product(normed_tokens, up_frozen_weight[:, span]).astype(jnp.bfloat16),
                cross_shard_total(cot_panel, down_frozen_weight[span]).astype(jnp.bfloat16),
            )
            if summed_chunks:
                partial, summed_chunks[-1] = lax.optimization_barrier((partial, summed_chunks[-1]))
            summed_chunks.append(lax.psum(partial, "row"))

        gate_low, up_low, gate_low_dir, up_low_dir, adj_low, adj_low_dir = [
            ranks[:, index * rank : (index + 1) * rank] for index in range(6)
        ]
        gate_pair = jnp.concatenate([gate_low_dir, gate_low], axis=1)
        up_pair = jnp.concatenate([up_low_dir, up_low], axis=1)
        adj_pair = jnp.concatenate([adj_low_dir, adj_low], axis=1)
        gate_stack = jnp.concatenate([gate_low_dir, gate_low], axis=0)
        up_stack = jnp.concatenate([up_low_dir, up_low], axis=0)
        adj_stack = jnp.concatenate([adj_low, adj_low_dir], axis=0)
        feature = 0.0
        gate_q = 0.0
        up_q = 0.0
        low_dir = 0.0
        gate_output, up_output, down_input = [], [], []
        for span, total in zip(spans, summed_chunks):
            gate_sum, up_sum, adj_sum = [value.astype(jnp.float32) for value in total]
            gate_pre = gate_sum + adapter_scale * curvature_product(
                gate_low, gate_output_factor[:, span]
            )
            up_pre = up_sum + adapter_scale * curvature_product(
                up_low, up_output_factor[:, span]
            )
            hidden_adj = adj_sum + adapter_scale * cross_shard_total(
                adj_low, down_input_factor[span]
            )
            gate_tan = adapter_scale * curvature_product(gate_pair, gate_out[:, span])
            up_tan = adapter_scale * curvature_product(up_pair, up_out[:, span])
            adj_tan = adapter_scale * cross_shard_total(adj_pair, down_in[span])
            hidden, hidden_dir, d_gate, d_up, d_gate_dir, d_up_dir = second_order(
                gate_pre, up_pre, hidden_adj, gate_tan, up_tan, adj_tan
            )
            gate_d = jnp.concatenate([d_gate, d_gate_dir], axis=0)
            up_d = jnp.concatenate([d_up, d_up_dir], axis=0)
            hidden_d = jnp.concatenate([hidden_dir, hidden], axis=0)
            gate_output.append(adapter_scale * summed_over_rows(gate_stack, gate_d))
            up_output.append(adapter_scale * summed_over_rows(up_stack, up_d))
            down_input.append(adapter_scale * summed_over_rows(hidden_d, adj_stack))
            gate_q = gate_q + cross_shard_total(gate_d, gate_out[:, span])
            up_q = up_q + cross_shard_total(up_d, up_out[:, span])
            low_dir = (
                low_dir
                + curvature_product(hidden_dir, down_input_factor[span])
                + curvature_product(hidden, down_input_factor_direction[span])
            )
            feature = (
                feature
                + cross_shard_total(gate_d, gate_frozen_weight[:, span])
                + cross_shard_total(up_d, up_frozen_weight[:, span])
            )
        gate_output = jnp.concatenate(gate_output, axis=1)
        up_output = jnp.concatenate(up_output, axis=1)
        down_input = jnp.concatenate(down_input, axis=0)

    summed = lax.psum_scatter(
        feature.astype(jnp.bfloat16).reshape(2, count, width_rows),
        "col",
        scatter_dimension=1,
        tiled=True,
    ).astype(jnp.float32)
    adjoints = shard_total(
        jnp.concatenate(
            [
                gate_q[:count, :rank],
                up_q[:count, :rank],
                gate_q[count:, :rank] + gate_q[:count, rank:],
                up_q[count:, :rank] + up_q[:count, rank:],
                low_dir,
            ],
            axis=1,
        ).astype(jnp.bfloat16),
        "col",
        1,
    )
    piece = lax.dynamic_slice_in_dim(adjoints, lax.axis_index("col") * own_count, own_count, 0)
    normed_feature_adjoint = summed[0] + adapter_scale * cross_shard_total(
        piece[:, : 2 * rank], in_factors[:, : 2 * rank]
    )
    normed_feature_adjoint_direction = summed[1] + adapter_scale * cross_shard_total(
        jnp.concatenate([piece[:, 2 * rank : 4 * rank], piece[:, : 2 * rank]], axis=1), in_factors
    )
    gate_input = adapter_scale * summed_over_rows(
        normed_tokens, adjoints[:, 2 * rank : 3 * rank]
    )
    up_input = adapter_scale * summed_over_rows(normed_tokens, adjoints[:, 3 * rank : 4 * rank])
    down_output = adapter_scale * summed_over_rows(adjoints[:, 4 * rank :], cot_panel)
    return (
        normed_feature_adjoint,
        normed_feature_adjoint_direction,
        gate_input,
        gate_output,
        up_input,
        up_output,
        down_input,
        down_output,
    )


def solution(mesh):
    in_specs = (
        P("col", "row"),
        P("row"),
        P("col", "row"),
        P("row", "col"),
        P("row", "col"),
        P("col", "row"),
        P("row", None),
        P(None, "col"),
        P("row", None),
        P(None, "col"),
        P("col", None),
        P(None, "row"),
        P("row", None),
        P(None, "col"),
        P("row", None),
        P(None, "col"),
        P("col", None),
        P(None, "row"),
    )
    out_specs = (
        P("col", "row"),
        P("col", "row"),
        P("row", None),
        P(None, "col"),
        P("row", None),
        P(None, "col"),
        P("col", None),
        P(None, "row"),
    )
    return jax.shard_map(
        on_device, mesh=mesh, in_specs=in_specs, out_specs=out_specs, check_vma=False
    )
```

```python
import functools

import jax
import jax.numpy as jnp
from jax import lax
from jax.experimental import pallas as pl
from jax.experimental.pallas import tpu as pltpu
from jax.sharding import PartitionSpec as P

adapter_scale = 0.5
epsilon = 1e-05
MESH = pl.DeviceIdType.MESH


def total_kernel(axis, n, x_ref, o_ref, inbox, whole, send1, recv1, send2, recv2):
    me = lax.axis_index(axis)
    barrier = pltpu.get_barrier_semaphore()

    @pl.loop(1, n)
    def _(k):
        pl.semaphore_signal(
            barrier, inc=1, device_id={axis: lax.rem(me + k, n)}, device_id_type=MESH
        )

    pl.semaphore_wait(barrier, n - 1)

    def scatter(k):
        peer = lax.rem(me + k, n)
        return pltpu.make_async_remote_copy(
            src_ref=x_ref.at[peer],
            dst_ref=inbox.at[k],
            send_sem=send1.at[k],
            recv_sem=recv1.at[k],
            device_id={axis: peer},
            device_id_type=MESH,
        )

    def spread(k):
        peer = lax.rem(me + k, n)
        return pltpu.make_async_remote_copy(
            src_ref=whole.at[me],
            dst_ref=whole.at[me],
            send_sem=send2.at[k],
            recv_sem=recv2.at[k],
            device_id={axis: peer},
            device_id_type=MESH,
        )

    def arrival(k):
        origin = lax.rem(me - k + n, n)
        return pltpu.make_async_remote_copy(
            src_ref=whole.at[origin],
            dst_ref=whole.at[origin],
            send_sem=send2.at[k],
            recv_sem=recv2.at[k],
            device_id={axis: origin},
            device_id_type=MESH,
        )

    @pl.loop(1, n)
    def _(k):
        scatter(k).start()

    def add(k, total):
        scatter(k).wait_recv()
        return total + inbox[k].astype(jnp.float32)

    total = lax.fori_loop(1, n, add, x_ref[me].astype(jnp.float32))
    whole[me] = total.astype(whole.dtype)

    @pl.loop(1, n)
    def _(k):
        spread(k).start()

    @pl.loop(1, n)
    def _(k):
        arrival(k).wait_recv()

    @pl.loop(1, n)
    def _(k):
        scatter(k).wait_send()
        spread(k).wait_send()

    o_ref[...] = whole[...]


def shard_total(x, axis, collective_id):
    n = lax.axis_size(axis)
    rows, columns = x.shape
    block = (n, rows // n, columns)
    total = pl.pallas_call(
        functools.partial(total_kernel, axis, n),
        out_shape=jax.ShapeDtypeStruct(block, jnp.bfloat16),
        in_specs=[pl.BlockSpec(memory_space=pltpu.VMEM)],
        out_specs=pl.BlockSpec(memory_space=pltpu.VMEM),
        scratch_shapes=[
            pltpu.VMEM(block, x.dtype),
            pltpu.VMEM(block, jnp.bfloat16),
            pltpu.SemaphoreType.DMA((n,)),
            pltpu.SemaphoreType.DMA((n,)),
            pltpu.SemaphoreType.DMA((n,)),
            pltpu.SemaphoreType.DMA((n,)),
        ],
        compiler_params=pltpu.CompilerParams(collective_id=collective_id, has_side_effects=True),
        name=f"total_{axis}",
    )(x.reshape(block))
    return total.reshape(rows, columns)


def curvature_product(left, right):
    return jnp.dot(left, right, preferred_element_type=jnp.float32)


def cross_shard_total(left, right):
    return lax.dot_general(
        left, right, (((1,), (1,)), ((), ())), preferred_element_type=jnp.float32
    )


def summed_over_rows(left, right):
    return lax.dot_general(
        left, right, (((0,), (0,)), ((), ())), preferred_element_type=jnp.float32
    )


def second_order(
    gate_preactivation,
    up_preactivation,
    hidden_adjoint,
    gate_tangent_rows,
    up_tangent_rows,
    adjoint_tangent_rows,
):
    sigma = jax.nn.sigmoid(gate_preactivation)
    silu_value = gate_preactivation * sigma
    slope = sigma * (1.0 + gate_preactivation * (1.0 - sigma))
    bend = sigma * (1.0 - sigma) * (2.0 + gate_preactivation * (1.0 - 2.0 * sigma))
    hidden_activation = (silu_value * up_preactivation).astype(jnp.bfloat16)
    hidden_direction = (
        slope * gate_tangent_rows * up_preactivation + silu_value * up_tangent_rows
    ).astype(jnp.bfloat16)
    gate_derivative = (hidden_adjoint * up_preactivation * slope).astype(jnp.bfloat16)
    up_derivative = (hidden_adjoint * silu_value).astype(jnp.bfloat16)
    gate_derivative_direction = (
        adjoint_tangent_rows * up_preactivation * slope
        + hidden_adjoint * (up_tangent_rows * slope + up_preactivation * bend * gate_tangent_rows)
    ).astype(jnp.bfloat16)
    up_derivative_direction = (
        adjoint_tangent_rows * silu_value + hidden_adjoint * slope * gate_tangent_rows
    ).astype(jnp.bfloat16)
    return (
        hidden_activation,
        hidden_direction,
        gate_derivative,
        up_derivative,
        gate_derivative_direction,
        up_derivative_direction,
    )


def block_kernel(
    x_ref,
    cot_ref,
    gate_hbm,
    up_hbm,
    down_hbm,
    gate_left,
    up_left,
    adj_left,
    gate_stack,
    up_stack,
    adj_stack,
    gate_out,
    up_out,
    down_in,
    feature_ref,
    gate_q,
    up_q,
    low_q,
    gate_curve,
    up_curve,
    down_curve,
    parts,
    first_in,
    second_out,
    second_in,
    whole,
    wide_buf,
    down_buf,
    total,
    send_sem,
    recv_sem,
    wide_sem,
    down_sem,
):
    me = lax.axis_index("row")
    flip_low = me + 1 - 2 * lax.rem(me, 2)
    flip_high = me + 2 - 4 * (me // 2)
    flip_both = 3 - me
    chunks, blocks, block, triple = parts.shape
    width = triple // 3
    count = x_ref.shape[0]
    depth = x_ref.shape[1]
    slots = wide_buf.shape[0]

    barrier = pltpu.get_barrier_semaphore()
    for peer in (flip_low, flip_high):
        pl.semaphore_signal(barrier, inc=1, device_id={"row": peer}, device_id_type=MESH)

    def lanes(c):
        return pl.ds(pl.multiple_of(c * width, width), width)

    def loads(c):
        slot, side = lax.rem(c, slots), lax.rem(c, 2)
        return [
            pltpu.make_async_copy(
                gate_hbm.at[:, lanes(c)], wide_buf.at[slot, 0], wide_sem.at[slot, 0]
            ),
            pltpu.make_async_copy(
                up_hbm.at[:, lanes(c)], wide_buf.at[slot, 1], wide_sem.at[slot, 1]
            ),
            pltpu.make_async_copy(down_hbm.at[lanes(c), :], down_buf.at[side], down_sem.at[side]),
        ]

    def send(src, dst, c, path, k, peer):
        return pltpu.make_async_remote_copy(
            src_ref=src,
            dst_ref=dst,
            send_sem=send_sem.at[c, path, k],
            recv_sem=recv_sem.at[c, path, k],
            device_id={"row": peer},
            device_id_type=MESH,
        )

    def ends(path):
        return (flip_low, flip_high) if path == 0 else (flip_high, flip_low)

    def sends(c, path, ks):
        near, far = ends(path)
        base = 4 * path
        table = [
            lambda: send(parts.at[c, base + near], first_in.at[c, path, 0], c, path, 0, near),
            lambda: send(parts.at[c, base + flip_both], first_in.at[c, path, 1], c, path, 1, near),
            lambda: send(second_out.at[c, path], second_in.at[c, path], c, path, 2, far),
            lambda: send(whole.at[c, base + me], whole.at[c, base + me], c, path, 3, far),
            lambda: send(whole.at[c, base + me], whole.at[c, base + me], c, path, 4, near),
            lambda: send(whole.at[c, base + far], whole.at[c, base + far], c, path, 5, near),
        ]
        return [table[k]() for k in ks]

    def arrivals(c, path, ks):
        near, far = ends(path)
        base = 4 * path
        table = [
            lambda: send(parts.at[c, base + me], first_in.at[c, path, 0], c, path, 0, near),
            lambda: send(parts.at[c, base + far], first_in.at[c, path, 1], c, path, 1, near),
            lambda: send(second_out.at[c, path], second_in.at[c, path], c, path, 2, far),
            lambda: send(whole.at[c, base + far], whole.at[c, base + far], c, path, 3, far),
            lambda: send(whole.at[c, base + near], whole.at[c, base + near], c, path, 4, near),
            lambda: send(whole.at[c, base + flip_both], whole.at[c, base + flip_both], c, path, 5, near),
        ]
        return [table[k]() for k in ks]

    def put(c, at, value):
        parts[c, :, :, at * width : (at + 1) * width] = value.astype(jnp.bfloat16).reshape(
            blocks, block, width
        )

    for copy in loads(0):
        copy.start()
    total[...] = jnp.zeros_like(total)
    gate_q[...] = jnp.zeros_like(gate_q)
    up_q[...] = jnp.zeros_like(up_q)
    low_q[...] = jnp.zeros_like(low_q)
    pl.semaphore_wait(barrier, 2)

    def project(c):
        for copy in loads(c):
            copy.wait()

        @pl.when(c + 1 < chunks)
        def _():
            for copy in loads(c + 1):
                copy.start()

        slot = lax.rem(c, slots)
        put(c, 0, curvature_product(x_ref[...], wide_buf[slot, 0]))
        put(c, 1, curvature_product(x_ref[...], wide_buf[slot, 1]))
        put(c, 2, cross_shard_total(cot_ref[...], down_buf[lax.rem(c, 2)]))
        for path in range(2):
            for copy in sends(c, path, (0, 1)):
                copy.start()

    def relay(c):
        for path in range(2):
            near, far = ends(path)
            for copy in arrivals(c, path, (0, 1)):
                copy.wait_recv()
            second_out[c, path] = (
                parts[c, 4 * path + far].astype(jnp.float32)
                + first_in[c, path, 1].astype(jnp.float32)
            ).astype(jnp.bfloat16)
            sends(c, path, (2,))[0].start()

    def settle(c):
        for path in range(2):
            arrivals(c, path, (2,))[0].wait_recv()
            whole[c, 4 * path + me] = (
                parts[c, 4 * path + me].astype(jnp.float32)
                + first_in[c, path, 0].astype(jnp.float32)
                + second_in[c, path].astype(jnp.float32)
            ).astype(jnp.bfloat16)
            for copy in sends(c, path, (3, 4)):
                copy.start()

    def forward(c):
        for path in range(2):
            arrivals(c, path, (3,))[0].wait_recv()
            sends(c, path, (5,))[0].start()

    def differentiate(c):
        for path in range(2):
            for copy in arrivals(c, path, (4, 5)):
                copy.wait_recv()

        def got(at):
            return (
                whole[c, :, :, at * width : (at + 1) * width]
                .reshape(count, width)
                .astype(jnp.float32)
            )

        gate_w, up_w, down_w = gate_out[:, lanes(c)], up_out[:, lanes(c)], down_in[lanes(c), :]
        gate_low = curvature_product(gate_left[...], gate_w)
        up_low = curvature_product(up_left[...], up_w)
        adj_low = cross_shard_total(adj_left[...], down_w)
        hidden, hidden_dir, d_gate, d_up, d_gate_dir, d_up_dir = second_order(
            got(0) + gate_low[:count],
            got(1) + up_low[:count],
            got(2) + adj_low[:count],
            gate_low[count:],
            up_low[count:],
            adj_low[count:],
        )
        gate_d = jnp.concatenate([d_gate, d_gate_dir], axis=0)
        up_d = jnp.concatenate([d_up, d_up_dir], axis=0)
        hidden_d = jnp.concatenate([hidden_dir, hidden], axis=0)
        gate_curve[:, lanes(c)] = curvature_product(gate_stack[...], gate_d)
        up_curve[:, lanes(c)] = curvature_product(up_stack[...], up_d)
        down_curve[:, lanes(c)] = curvature_product(adj_stack[...], hidden_d)
        gate_q[...] += cross_shard_total(gate_d, gate_w)
        up_q[...] += cross_shard_total(up_d, up_w)
        low_q[...] += curvature_product(hidden_d, down_w)
        slot = lax.rem(c, slots)
        piece = 512 if depth % 512 == 0 else depth
        for start in range(0, depth, piece):
            span = slice(start, start + piece)
            total[:, span] += cross_shard_total(
                gate_d, wide_buf[slot, 0, span, :]
            ) + cross_shard_total(up_d, wide_buf[slot, 1, span, :])

    @pl.loop(0, chunks + 4)
    def _(t):
        for lag, stage in enumerate((project, relay, settle, forward, differentiate)):

            @pl.when((t >= lag) & (t < chunks + lag))
            def _(lag=lag, stage=stage):
                stage(t - lag)

    @pl.loop(0, chunks)
    def _(c):
        for path in range(2):
            for copy in sends(c, path, range(6)):
                copy.wait_send()

    feature_ref[...] = total[...].astype(jnp.bfloat16)


def fused_block(x, cot, gate_w, up_w, down_w, ranks, gate_out, up_out, down_in, width):
    count, depth = x.shape
    columns = gate_w.shape[1]
    rank = ranks.shape[1] // 6
    chunks = columns // width
    half = ranks * adapter_scale
    gate, up, gate_dir, up_dir, adj, adj_dir = [
        half[:, index * rank : (index + 1) * rank] for index in range(6)
    ]
    empty = jnp.zeros_like(gate)

    def left(low, low_dir):
        return jnp.concatenate(
            [
                jnp.concatenate([low, empty], axis=1),
                jnp.concatenate([low_dir, low], axis=1),
            ],
            axis=0,
        )

    vmem = pl.BlockSpec(memory_space=pltpu.VMEM)
    anywhere = pl.BlockSpec(memory_space=pl.ANY)
    block = count // 8
    f32, bf16 = jnp.float32, jnp.bfloat16
    return pl.pallas_call(
        block_kernel,
        out_shape=[
            jax.ShapeDtypeStruct((2 * count, depth), bf16),
            jax.ShapeDtypeStruct((2 * count, 2 * rank), f32),
            jax.ShapeDtypeStruct((2 * count, 2 * rank), f32),
            jax.ShapeDtypeStruct((2 * count, 2 * rank), f32),
            jax.ShapeDtypeStruct((rank, columns), f32),
            jax.ShapeDtypeStruct((rank, columns), f32),
            jax.ShapeDtypeStruct((rank, columns), f32),
        ],
        in_specs=[vmem] * 2 + [anywhere] * 3 + [vmem] * 9,
        out_specs=[vmem] * 7,
        scratch_shapes=[
            pltpu.VMEM((chunks, 8, block, 3 * width), bf16),
            pltpu.VMEM((chunks, 2, 2, block, 3 * width), bf16),
            pltpu.VMEM((chunks, 2, block, 3 * width), bf16),
            pltpu.VMEM((chunks, 2, block, 3 * width), bf16),
            pltpu.VMEM((chunks, 8, block, 3 * width), bf16),
            pltpu.VMEM((6, 2, depth, width), bf16),
            pltpu.VMEM((2, width, depth), bf16),
            pltpu.VMEM((2 * count, depth), f32),
            pltpu.SemaphoreType.DMA((chunks, 2, 6)),
            pltpu.SemaphoreType.DMA((chunks, 2, 6)),
            pltpu.SemaphoreType.DMA((6, 2)),
            pltpu.SemaphoreType.DMA((2,)),
        ],
        compiler_params=pltpu.CompilerParams(
            collective_id=2, has_side_effects=True, vmem_limit_bytes=60 * 1024 * 1024
        ),
        name="block",
    )(
        x,
        cot,
        gate_w,
        up_w,
        down_w,
        left(gate, gate_dir),
        left(up, up_dir),
        left(adj, adj_dir),
        jnp.concatenate([gate_dir, gate], axis=0).T,
        jnp.concatenate([up_dir, up], axis=0).T,
        jnp.concatenate([adj, adj_dir], axis=0).T,
        gate_out,
        up_out,
        down_in,
    )


def gather_kernel(
    tokens,
    gain,
    cot,
    x_all,
    cot_all,
    x_buf,
    cot_buf,
    squares,
    square_send,
    square_recv,
    far_send,
    far_recv,
    near_send,
    near_recv,
):
    rows, columns = lax.axis_size("row"), lax.axis_size("col")
    chips = columns // 2
    my_row, me = lax.axis_index("row"), lax.axis_index("col")
    partner = me + 1 - 2 * lax.rem(me, 2)
    features = rows * tokens.shape[1]
    barrier = pltpu.get_barrier_semaphore()

    def row_peer(k):
        return {"row": lax.rem(my_row + k, rows)}

    def far_peer(k):
        return {"col": lax.rem(me + 2 * k, columns)}

    @pl.loop(1, rows)
    def _(k):
        pl.semaphore_signal(barrier, inc=1, device_id=row_peer(k), device_id_type=MESH)

    @pl.loop(1, chips)
    def _(k):
        pl.semaphore_signal(barrier, inc=1, device_id=far_peer(k), device_id_type=MESH)

    pl.semaphore_signal(barrier, inc=1, device_id={"col": partner}, device_id_type=MESH)

    buffers = (cot_buf, x_buf)

    def origin(k):
        return lax.rem(me - 2 * k + columns, columns)

    def square(k):
        return pltpu.make_async_remote_copy(
            src_ref=squares.at[0],
            dst_ref=squares.at[k],
            send_sem=square_send.at[k],
            recv_sem=square_recv.at[k],
            device_id=row_peer(k),
            device_id_type=MESH,
        )

    def far(which, k, slot):
        return pltpu.make_async_remote_copy(
            src_ref=buffers[which].at[slot],
            dst_ref=buffers[which].at[slot],
            send_sem=far_send.at[which, k],
            recv_sem=far_recv.at[which, k],
            device_id=far_peer(k),
            device_id_type=MESH,
        )

    def near(which, k, slot):
        return pltpu.make_async_remote_copy(
            src_ref=buffers[which].at[slot],
            dst_ref=buffers[which].at[slot],
            send_sem=near_send.at[which, k],
            recv_sem=near_recv.at[which, k],
            device_id={"col": partner},
            device_id_type=MESH,
        )

    def launch(which):
        @pl.loop(1, chips)
        def _(k):
            far(which, k, me).start()

        near(which, 0, me).start()

    values = tokens[...].astype(jnp.float32)
    squares[0] = jnp.broadcast_to(
        jnp.sum(values * values, axis=1, keepdims=True), squares.shape[1:]
    )
    cot_buf[me] = cot[...]
    pl.semaphore_wait(barrier, rows + chips - 1)

    @pl.loop(1, rows)
    def _(k):
        square(k).start()

    launch(0)

    def add(k, total):
        square(k).wait_recv()
        return total + squares[k]

    total = lax.fori_loop(1, rows, add, squares[0])
    scale = lax.rsqrt(total[:, :1] / features + epsilon)
    x_buf[me] = (tokens[...].astype(jnp.float32) * scale * gain[...]).astype(jnp.bfloat16)
    launch(1)
    for which in range(2):

        @pl.loop(1, chips)
        def _(k, which=which):
            far(which, k, origin(k)).wait_recv()
            near(which, k, origin(k)).start()

    for which in range(2):

        @pl.loop(0, chips)
        def _(k, which=which):
            near(which, k, lax.rem(partner - 2 * k + columns, columns)).wait_recv()

    @pl.loop(1, rows)
    def _(k):
        square(k).wait_send()

    for which in range(2):

        @pl.loop(1, chips)
        def _(k, which=which):
            far(which, k, me).wait_send()

        @pl.loop(0, chips)
        def _(k, which=which):
            near(which, k, origin(k)).wait_send()

    cot_all[...] = cot_buf[...]
    x_all[...] = x_buf[...]


def gathered(tokens, gain, cot):
    rows, columns = lax.axis_size("row"), lax.axis_size("col")
    own, depth = tokens.shape
    whole = (columns, own, depth)
    vmem = pl.BlockSpec(memory_space=pltpu.VMEM)
    x, panel = pl.pallas_call(
        gather_kernel,
        out_shape=[jax.ShapeDtypeStruct(whole, jnp.bfloat16)] * 2,
        in_specs=[vmem] * 3,
        out_specs=[vmem] * 2,
        scratch_shapes=[
            pltpu.VMEM(whole, jnp.bfloat16),
            pltpu.VMEM(whole, jnp.bfloat16),
            pltpu.VMEM((rows, own, 128), jnp.float32),
            pltpu.SemaphoreType.DMA((rows,)),
            pltpu.SemaphoreType.DMA((rows,)),
            pltpu.SemaphoreType.DMA((2, columns // 2)),
            pltpu.SemaphoreType.DMA((2, columns // 2)),
            pltpu.SemaphoreType.DMA((2, columns // 2)),
            pltpu.SemaphoreType.DMA((2, columns // 2)),
        ],
        compiler_params=pltpu.CompilerParams(collective_id=3, has_side_effects=True),
        name="gather",
    )(tokens, gain.reshape(1, depth), cot)
    return x.reshape(columns * own, depth), panel.reshape(columns * own, depth)


def chunk_count(width):
    for count in (4, 2):
        if width % (128 * count) == 0:
            return count
    return 1


def on_device(
    tokens,
    norm_gain,
    cotangent,
    gate_frozen_weight,
    up_frozen_weight,
    down_frozen_weight,
    gate_input_factor,
    gate_output_factor,
    up_input_factor,
    up_output_factor,
    down_input_factor,
    down_b,
    gate_input_factor_direction,
    gate_output_factor_direction,
    up_input_factor_direction,
    up_output_factor_direction,
    down_input_factor_direction,
    down_b_dir,
):
    rank = gate_input_factor.shape[1]
    width_rows, width_columns = gate_frozen_weight.shape
    own_count = tokens.shape[0]
    normed_tokens, cot_panel = gathered(tokens, norm_gain, cotangent)
    count = normed_tokens.shape[0]
    in_factors = jnp.concatenate(
        [
            gate_input_factor,
            up_input_factor,
            gate_input_factor_direction,
            up_input_factor_direction,
        ],
        axis=1,
    )
    out_factors = jnp.concatenate([down_b, down_b_dir], axis=0)

    projected = jnp.concatenate(
        [curvature_product(normed_tokens, in_factors), cross_shard_total(cot_panel, out_factors)],
        axis=1,
    )
    ranks = shard_total(projected.astype(jnp.bfloat16), "row", 0)
    gate_out = jnp.concatenate([gate_output_factor, gate_output_factor_direction], axis=0)
    up_out = jnp.concatenate([up_output_factor, up_output_factor_direction], axis=0)
    down_in = jnp.concatenate([down_input_factor, down_input_factor_direction], axis=1)

    width = 256
    if lax.axis_size("row") == 4 and width_columns % width == 0 and count % 128 == 0:
        feature, gate_q, up_q, low_q, gate_output, up_output, down_input = fused_block(
            normed_tokens,
            cot_panel,
            gate_frozen_weight,
            up_frozen_weight,
            down_frozen_weight,
            ranks,
            gate_out,
            up_out,
            down_in,
            width,
        )
        low_dir = low_q[:count, :rank] + low_q[count:, rank:]
        down_input = down_input.T
    else:
        chunks = chunk_count(width_columns)
        wide = width_columns // chunks
        spans = [slice(index * wide, (index + 1) * wide) for index in range(chunks)]

        summed_chunks = []
        for span in spans:
            partial = (
                curvature_product(normed_tokens, gate_frozen_weight[:, span]).astype(jnp.bfloat16),
                curvature_product(normed_tokens, up_frozen_weight[:, span]).astype(jnp.bfloat16),
                cross_shard_total(cot_panel, down_frozen_weight[span]).astype(jnp.bfloat16),
            )
            if summed_chunks:
                partial, summed_chunks[-1] = lax.optimization_barrier((partial, summed_chunks[-1]))
            summed_chunks.append(lax.psum(partial, "row"))

        gate_low, up_low, gate_low_dir, up_low_dir, adj_low, adj_low_dir = [
            ranks[:, index * rank : (index + 1) * rank] for index in range(6)
        ]
        gate_pair = jnp.concatenate([gate_low_dir, gate_low], axis=1)
        up_pair = jnp.concatenate([up_low_dir, up_low], axis=1)
        adj_pair = jnp.concatenate([adj_low_dir, adj_low], axis=1)
        gate_stack = jnp.concatenate([gate_low_dir, gate_low], axis=0)
        up_stack = jnp.concatenate([up_low_dir, up_low], axis=0)
        adj_stack = jnp.concatenate([adj_low, adj_low_dir], axis=0)
        feature = 0.0
        gate_q = 0.0
        up_q = 0.0
        low_dir = 0.0
        gate_output, up_output, down_input = [], [], []
        for span, total in zip(spans, summed_chunks):
            gate_sum, up_sum, adj_sum = [value.astype(jnp.float32) for value in total]
            gate_pre = gate_sum + adapter_scale * curvature_product(
                gate_low, gate_output_factor[:, span]
            )
            up_pre = up_sum + adapter_scale * curvature_product(
                up_low, up_output_factor[:, span]
            )
            hidden_adj = adj_sum + adapter_scale * cross_shard_total(
                adj_low, down_input_factor[span]
            )
            gate_tan = adapter_scale * curvature_product(gate_pair, gate_out[:, span])
            up_tan = adapter_scale * curvature_product(up_pair, up_out[:, span])
            adj_tan = adapter_scale * cross_shard_total(adj_pair, down_in[span])
            hidden, hidden_dir, d_gate, d_up, d_gate_dir, d_up_dir = second_order(
                gate_pre, up_pre, hidden_adj, gate_tan, up_tan, adj_tan
            )
            gate_d = jnp.concatenate([d_gate, d_gate_dir], axis=0)
            up_d = jnp.concatenate([d_up, d_up_dir], axis=0)
            hidden_d = jnp.concatenate([hidden_dir, hidden], axis=0)
            gate_output.append(adapter_scale * summed_over_rows(gate_stack, gate_d))
            up_output.append(adapter_scale * summed_over_rows(up_stack, up_d))
            down_input.append(adapter_scale * summed_over_rows(hidden_d, adj_stack))
            gate_q = gate_q + cross_shard_total(gate_d, gate_out[:, span])
            up_q = up_q + cross_shard_total(up_d, up_out[:, span])
            low_dir = (
                low_dir
                + curvature_product(hidden_dir, down_input_factor[span])
                + curvature_product(hidden, down_input_factor_direction[span])
            )
            feature = (
                feature
                + cross_shard_total(gate_d, gate_frozen_weight[:, span])
                + cross_shard_total(up_d, up_frozen_weight[:, span])
            )
        gate_output = jnp.concatenate(gate_output, axis=1)
        up_output = jnp.concatenate(up_output, axis=1)
        down_input = jnp.concatenate(down_input, axis=0)

    summed = lax.psum_scatter(
        feature.astype(jnp.bfloat16).reshape(2, count, width_rows),
        "col",
        scatter_dimension=1,
        tiled=True,
    ).astype(jnp.float32)
    adjoints = shard_total(
        jnp.concatenate(
            [
                gate_q[:count, :rank],
                up_q[:count, :rank],
                gate_q[count:, :rank] + gate_q[:count, rank:],
                up_q[count:, :rank] + up_q[:count, rank:],
                low_dir,
            ],
            axis=1,
        ).astype(jnp.bfloat16),
        "col",
        1,
    )
    piece = lax.dynamic_slice_in_dim(adjoints, lax.axis_index("col") * own_count, own_count, 0)
    normed_feature_adjoint = summed[0] + adapter_scale * cross_shard_total(
        piece[:, : 2 * rank], in_factors[:, : 2 * rank]
    )
    normed_feature_adjoint_direction = summed[1] + adapter_scale * cross_shard_total(
        jnp.concatenate([piece[:, 2 * rank : 4 * rank], piece[:, : 2 * rank]], axis=1), in_factors
    )
    gate_input = adapter_scale * summed_over_rows(
        normed_tokens, adjoints[:, 2 * rank : 3 * rank]
    )
    up_input = adapter_scale * summed_over_rows(normed_tokens, adjoints[:, 3 * rank : 4 * rank])
    down_output = adapter_scale * summed_over_rows(adjoints[:, 4 * rank :], cot_panel)
    return (
        normed_feature_adjoint,
        normed_feature_adjoint_direction,
        gate_input,
        gate_output,
        up_input,
        up_output,
        down_input,
        down_output,
    )


def solution(mesh):
    in_specs = (
        P("col", "row"),
        P("row"),
        P("col", "row"),
        P("row", "col"),
        P("row", "col"),
        P("col", "row"),
        P("row", None),
        P(None, "col"),
        P("row", None),
        P(None, "col"),
        P("col", None),
        P(None, "row"),
        P("row", None),
        P(None, "col"),
        P("row", None),
        P(None, "col"),
        P("col", None),
        P(None, "row"),
    )
    out_specs = (
        P("col", "row"),
        P("col", "row"),
        P("row", None),
        P(None, "col"),
        P("row", None),
        P(None, "col"),
        P("col", None),
        P(None, "row"),
    )
    return jax.shard_map(
        on_device, mesh=mesh, in_specs=in_specs, out_specs=out_specs, check_vma=False
    )
```
